128 devices in a mesh: fsdp: 16 (over y_hi, z, core), tp: 8 (over x, y_lo).
Axes of the slice: x: 4, y: 4 (y_hi: 2, y_lo: 2; y = y_hi * 2 + y_lo), z: 4, core: 2. Of those that a mesh axis runs over, the one named last changes fastest.
Arguments:
- tokens: bfloat16 [12288, 4096], P('fsdp', 'tp'), may hold values from -14 to 14
- target: bfloat16 [12288, 4096], P('fsdp', 'tp'), may hold values from -6 to 6
- w_query: bfloat16 [4096, 4096], P('fsdp', 'tp'), may hold values from -0.09375 to 0.09375
- w_key: bfloat16 [4096, 1024], P('fsdp', 'tp'), may hold values from -0.09375 to 0.09375
- w_value: bfloat16 [4096, 1024], P('fsdp', 'tp'), may hold values from -0.09375 to 0.09375
- t_query: bfloat16 [4096, 4096], P('fsdp', 'tp'), may hold values from -0.09375 to 0.09375
- t_key: bfloat16 [4096, 1024], P('fsdp', 'tp'), may hold values from -0.09375 to 0.09375
- t_value: bfloat16 [4096, 1024], P('fsdp', 'tp'), may hold values from -0.09375 to 0.09375
Outputs:
- curve_query: float32 [4096, 4096], P('fsdp', 'tp')
- curve_key: float32 [4096, 1024], P('fsdp', 'tp')
- curve_value: float32 [4096, 1024], P('fsdp', 'tp')
The draws below stay inside these ranges and needn't reach their ends.
All inputs are finite; a program needn't handle non-finite values.
Results may differ from the reference program's by a relative error of at most 0.03.
The reference program's roundings to bfloat16 on the way count: a program that leaves them out, or rounds other values in their place, can miss the bound.
Values may be sent and summed in bfloat16 or wider, within the bound.
A program may use at most 64 MiB of HBM per device.

```python
import math
import jax
import jax.numpy as jnp
from jax import lax

D = 4096
QH = 32
KVH = 8
HD = 128
TOK_DEV = 768
TOKENS = 12288


def draw_tokens(key, part):
    return jax.random.truncated_normal(key, -4.0, 4.0, (TOKENS, D), jnp.float32).astype(jnp.bfloat16)


def block_levels(stream_key, shape, shards, low, largest):
    def one(dim, parts):
        draws = jax.random.uniform(jax.random.fold_in(jax.random.fold_in(stream_key, 6), dim), (parts,), jnp.float32, low / len(shards), largest / len(shards))
        return jnp.repeat(jnp.exp(draws), shape[dim] // parts).reshape((-1,) + (1,) * (len(shape) - dim - 1))

    loudness = one(*shards[0])
    for cut in shards[1:]:
        loudness = loudness * one(*cut)
    return loudness


def noise(stream_key, dims, deviation, reach, shards=(), kind=jnp.bfloat16):
    factor_of = block_levels(stream_key, dims, shards, -0.22, 0.18) if shards else 1.0
    entries = jax.random.normal(stream_key, dims, jnp.float32) * deviation * factor_of
    return jnp.minimum(jnp.maximum(entries, -reach), reach).astype(kind)


def setup_inputs(seed: int = 0) -> dict:
    splits = jax.random.split(jax.random.key(seed), 9)
    return {
        "tokens": draw_tokens(jax.random.fold_in(splits[8], 71), 0),
        "target": noise(splits[1], (TOKENS, QH * HD), 1.0, 6.0, ((0, 16), (1, 8))),
        "w_query": noise(splits[2], (D, QH * HD), D ** -0.5, 0.09375, ((0, 16), (1, 8))),
        "w_key": noise(splits[3], (D, KVH * HD), D ** -0.5, 0.09375, ((0, 16), (1, 8))),
        "w_value": noise(splits[4], (D, KVH * HD), D ** -0.5, 0.09375, ((0, 16), (1, 8))),
        "t_query": noise(splits[5], (D, QH * HD), D ** -0.5, 0.09375, ((0, 16), (1, 8))),
        "t_key": noise(splits[6], (D, KVH * HD), D ** -0.5, 0.09375, ((0, 16), (1, 8))),
        "t_value": noise(splits[7], (D, KVH * HD), D ** -0.5, 0.09375, ((0, 16), (1, 8))),
    }


def rope_tables(length, width):
    halfway = width // 2
    frequency = jnp.exp(jnp.arange(halfway, dtype=jnp.float32) * (-2.0 * math.log(10000.0) / width))
    angles = jnp.arange(length, dtype=jnp.float32)[:, None] * frequency[None, :]
    return (jnp.cos(angles), jnp.sin(angles))

def rotate(inputs, cosine_table, sine_table):
    halfway = inputs.shape[1] // 2
    leading = inputs[:, :halfway]
    trailing = inputs[:, halfway:]
    return jnp.concatenate([leading * cosine_table - trailing * sine_table, trailing * cosine_table + leading * sine_table], axis=1)

def head_loss(query_head, key_head, value_head, target_head, cosine_table, sine_table, factor):
    length = query_head.shape[0]
    rotated_query = rotate(query_head, cosine_table, sine_table).astype(jnp.bfloat16)
    rotated_key = rotate(key_head, cosine_table, sine_table).astype(jnp.bfloat16)
    value_low = value_head.astype(jnp.bfloat16)
    scores = jnp.dot(rotated_query, rotated_key.T, preferred_element_type=jnp.float32) * query_head.shape[1] ** (-0.5)
    position = lax.broadcasted_iota(jnp.int32, (length, length), 0)
    earlier = lax.broadcasted_iota(jnp.int32, (length, length), 1)
    scores = jnp.where(earlier <= position, scores, -1e+30)
    weights = jax.nn.softmax(scores, axis=-1).astype(jnp.bfloat16)
    mixture = jnp.dot(weights, value_low, preferred_element_type=jnp.float32)
    mismatch = mixture - target_head.astype(jnp.float32)
    return 0.5 * factor * jnp.sum(mismatch * mismatch)

def group_curvature(query_group, key_group, value_group, tangent_query, tangent_key, tangent_value, target_group, cosine_table, sine_table, factor):

    def one_head(running, packed):
        query_head, tangent_head, target_head = packed

        def gradient(query_in, key_in, value_in):
            return jax.grad(head_loss, argnums=(0, 1, 2))(query_in, key_in, value_in, target_head, cosine_table, sine_table, factor)
        ignored, derived = jax.jvp(gradient, (query_head, key_group, value_group), (tangent_head, tangent_key, tangent_value))
        return ((running[0] + derived[1], running[1] + derived[2]), derived[0])
    blank_sum = jnp.zeros(key_group.shape, jnp.float32)
    packed_all = (jnp.moveaxis(query_group, 1, 0), jnp.moveaxis(tangent_query, 1, 0), jnp.moveaxis(target_group, 1, 0))
    totals, per_head = lax.scan(one_head, (blank_sum, blank_sum), packed_all)
    return (jnp.moveaxis(per_head, 0, 1), totals[0], totals[1])

def local_curvature(query, key_rows, value_rows, d_query, d_key, d_value, target_rows, factor, group_size, head_width):
    length = query.shape[0]
    cosine_table, sine_table = rope_tables(length, head_width)
    group_count = key_rows.shape[1] // head_width
    block_width = group_size * head_width
    query_parts, key_parts, value_parts = ([], [], [])
    for member in range(group_count):
        wide_lo = member * block_width
        wide_hi = wide_lo + block_width
        narrow_lo = member * head_width
        narrow_hi = narrow_lo + head_width
        dual_query, dual_key, dual_value = group_curvature(query[:, wide_lo:wide_hi].reshape(length, group_size, head_width), key_rows[:, narrow_lo:narrow_hi], value_rows[:, narrow_lo:narrow_hi], d_query[:, wide_lo:wide_hi].reshape(length, group_size, head_width), d_key[:, narrow_lo:narrow_hi], d_value[:, narrow_lo:narrow_hi], target_rows[:, wide_lo:wide_hi].reshape(length, group_size, head_width), cosine_table, sine_table, factor)
        query_parts.append(dual_query.reshape(length, block_width))
        key_parts.append(dual_key)
        value_parts.append(dual_value)
    low_query = jnp.concatenate(query_parts, axis=1).astype(jnp.bfloat16)
    low_key = jnp.concatenate(key_parts, axis=1).astype(jnp.bfloat16)
    low_value = jnp.concatenate(value_parts, axis=1).astype(jnp.bfloat16)
    return (low_query, low_key, low_value)

def rounded_part(sequence_rows, dual_low):
    term = lax.dot_general(sequence_rows, dual_low, (((0,), (0,)), ((), ())), preferred_element_type=jnp.float32)
    return lax.optimization_barrier(term.astype(jnp.bfloat16)).astype(jnp.float32)

def reference(tokens, target, w_query, w_key, w_value, t_query, t_key, t_value):
    factor = TOKENS ** (-0.5)

    def one_sequence(running, number):
        offset = number * TOK_DEV
        sequence_rows = lax.dynamic_slice_in_dim(tokens, offset, TOK_DEV, 0)
        wanted = lax.dynamic_slice_in_dim(target, offset, TOK_DEV, 0)
        projected = [jnp.dot(sequence_rows, weight, preferred_element_type=jnp.float32) for weight in (w_query, w_key, w_value, t_query, t_key, t_value)]
        cotangents = local_curvature(projected[0], projected[1], projected[2], projected[3], projected[4], projected[5], wanted, factor, QH // KVH, HD)
        updated = tuple((total_in + rounded_part(sequence_rows, dual_low) for total_in, dual_low in zip(running, cotangents)))
        return (updated, None)
    initial = (jnp.zeros((D, QH * HD), jnp.float32), jnp.zeros((D, KVH * HD), jnp.float32), jnp.zeros((D, KVH * HD), jnp.float32))
    result, ignored = lax.scan(one_sequence, initial, jnp.arange(TOKENS // TOK_DEV, dtype=jnp.int32))
    return (result[0], result[1], result[2])
```

```python
import functools
import math

import jax
import jax.numpy as jnp
import numpy as np
from jax import lax
from jax.experimental import pallas as pl
from jax.experimental.pallas import tpu as pltpu
from jax.sharding import PartitionSpec as P

MESH = pl.DeviceIdType.MESH
BF = jnp.bfloat16
F32 = jnp.float32

HD = 128
T = 768
D = 4096
HEADS = 4
R = 256
COLS = 1536
SIGMA = HD ** (-0.5)
LOG2E = 1.4426950408889634


def rope_tables(length, width):
    halfway = width // 2
    frequency = np.exp(np.arange(halfway, dtype=np.float32) * np.float32(-2.0 * math.log(10000.0) / width)).astype(np.float32)
    angles = np.arange(length, dtype=np.float32)[:, None] * frequency[None, :]
    angles = angles.astype(np.float64)
    return np.cos(angles).astype(np.float32), np.sin(angles).astype(np.float32)


def dot(a, b):
    return jnp.dot(a, b, preferred_element_type=F32)


def dot_nt(a, b):
    return lax.dot_general(a, b, (((1,), (1,)), ((), ())), preferred_element_type=F32)


def rope(u, cc, ss):
    return u * cc + pltpu.roll(u, HD // 2, 1) * ss


def unrope(u, cc, ss):
    return u * cc - pltpu.roll(u, HD // 2, 1) * ss


def prepare(project, cc_ref, ss_ref, q2, q2t, k2, v2):
    for i in range(T // R):
        rows = slice(i * R, (i + 1) * R)
        cc, ss = cc_ref[rows, :], ss_ref[rows, :]
        k2[rows, :HD] = rope(project("key", 0, rows), cc, ss).astype(BF)
        k2[rows, HD:] = rope(project("d_key", 0, rows), cc, ss).astype(BF)
        v2[rows, :HD] = project("value", 0, rows).astype(BF)
        v2[rows, HD:] = (project("d_value", 0, rows) * (1.0 / SIGMA)).astype(BF)

    def one(h, carry):
        for i in range(T // R):
            rows = slice(i * R, (i + 1) * R)
            cc, ss = cc_ref[rows, :], ss_ref[rows, :]
            both = jnp.concatenate(
                [
                    rope(project("d_query", h, rows), cc, ss),
                    rope(project("query", h, rows), cc, ss),
                ],
                axis=1,
            )
            q2[h, rows, :] = both.astype(BF)
            q2t[h, :, rows] = both.T.astype(BF)
        return carry

    lax.fori_loop(0, HEADS, one, 0)


def block(h, i, factor, q2, q2t, k2, v2, target, cc_ref, ss_ref, dk1, dk2, dvt, lowt):
    rows = slice(i * R, (i + 1) * R)
    width = (i + 1) * R
    q_both = q2[h, rows, :]
    kr, kd = k2[:width, :HD], k2[:width, HD:]
    vr = v2[:width, :HD]
    s = dot_nt(q_both[:, HD:], kr)
    ds = dot_nt(q_both, k2[:width, :])
    row = lax.broadcasted_iota(jnp.int32, (R, R), 0)
    col = lax.broadcasted_iota(jnp.int32, (R, R), 1)
    last = jnp.where(col <= row, s[:, i * R:], -1e30)
    s = last if i == 0 else jnp.concatenate([s[:, : i * R], last], axis=1)
    top = jnp.max(s, axis=1, keepdims=True)
    e = jnp.exp2((s - top) * (SIGMA * LOG2E))
    p = e * (1.0 / jnp.sum(e, axis=1, keepdims=True))
    w = ds - jnp.sum(p * ds, axis=1, keepdims=True)
    pd = p * w
    pb, pdb = p.astype(BF), pd.astype(BF)
    mixed = dot(pb, v2[:width, :])
    mix = mixed[:, :HD]
    dmix = dot(pdb, vr) + mixed[:, HD:]
    err = (mix - target(h, rows).astype(F32)) * factor
    derr = dmix * factor
    both = jnp.concatenate([derr, err], axis=1)
    both_low = both.astype(BF)
    both_t = both.T.astype(BF)
    dp = dot_nt(both_low[:, HD:], vr)
    ddp = dot_nt(both_low, v2[:width, :])
    delta = jnp.sum(err * mix, axis=1, keepdims=True)
    ddelta = jnp.sum(derr * mix + err * dmix, axis=1, keepdims=True)
    g = dp - delta
    gs = (p * g).astype(BF)
    gd = (p * (w * g + (ddp - ddelta))).astype(BF)
    dq = dot(gd, kr) * (SIGMA * SIGMA) + dot(gs, kd) * SIGMA
    dq = unrope(dq.astype(BF).astype(F32), cc_ref[rows, :], ss_ref[rows, :])
    lowt[h, :, rows] = dq.T.astype(BF)
    dvt[:, :width] += dot(both_t[HD:], pdb) + dot(both_t[:HD], pb)
    dk1[:, :width] += dot(q2t[h, HD:, rows], gd)
    dk2[:, :width] += dot(q2t[h, :HD, rows], gs)


def clear(dk1, dk2, dvt):
    for ref in (dk1, dk2, dvt):
        ref[...] = jnp.zeros(ref.shape, F32)


def finish_key(cct_ref, sst_ref, dk1, dk2, dvt, lowt):
    dk = dk1[...] * (SIGMA * SIGMA) + dk2[...] * SIGMA
    a, b = dk[: HD // 2], dk[HD // 2:]
    ct, st = cct_ref[...], sst_ref[...]
    lowt[HEADS, : HD // 2, :] = (a * ct + b * st).astype(BF)
    lowt[HEADS, HD // 2:, :] = (b * ct - a * st).astype(BF)
    lowt[HEADS + 1] = (dvt[...] * SIGMA).astype(BF)


def barrier(peers):
    sem = pltpu.get_barrier_semaphore()
    for peer in peers:
        pl.semaphore_signal(sem, inc=1, device_id=peer, device_id_type=MESH)
    pl.semaphore_wait(sem, len(peers))


def remote(src, dst, send, recv, peer):
    return pltpu.make_async_remote_copy(
        src_ref=src, dst_ref=dst, send_sem=send, recv_sem=recv, device_id=peer, device_id_type=MESH
    )


class Place:
    def __init__(self):
        self.f = lax.axis_index("fsdp")
        self.t = lax.axis_index("tp")
        self.core = lax.rem(self.f, 2)
        self.z = lax.rem(lax.div(self.f, 2), 4)
        self.yh = lax.div(self.f, 8)
        self.x = lax.div(self.t, 2)
        self.y = lax.rem(self.t, 2)

    def along(self, base, step):
        return lax.rem(base + step, 4)

    def fsdp(self, yh, z, core):
        return {"fsdp": (yh * 4 + z) * 2 + core, "tp": self.t}

    def tp(self, x, y):
        return {"fsdp": self.f, "tp": x * 2 + y}


class Ring:
    def __init__(self, r, p, slot, peer, own, send, recv):
        self.slot, self.own, self.send, self.recv = slot, own, send, recv
        right, left, far, q = lax.rem(r + 1, 4), lax.rem(r + 3, 4), lax.rem(r + 2, 4), 1 - p
        to_right, to_left, to_pair = peer(right, p), peer(left, p), peer(r, q)
        self.kinds = [
            ((r, p), 0, to_right, (left, p)),
            ((r, p), 0, to_left, (right, p)),
            ((r, p), 0, to_pair, (r, q)),
            ((left, p), 1, to_right, (far, p)),
            ((right, p), 2, to_left, (far, p)),
            ((r, q), 0, to_right, (left, q)),
            ((r, q), 0, to_left, (right, q)),
            ((left, q), 1, to_right, (far, q)),
            ((right, q), 2, to_left, (far, q)),
        ]

    def make(self, kind):
        chunk, part, to, _ = self.kinds[kind]
        src = self.own if kind < 3 else self.slot(*chunk, part)
        return remote(src, self.slot(*chunk, part), self.send.at[kind], self.recv.at[kind], to)

    def start(self, kind):
        self.make(kind).start()

    def wait_recv(self, kind):
        _, part, to, arrives = self.kinds[kind]
        ref = self.slot(*arrives, part)
        remote(ref, ref, self.send.at[kind], self.recv.at[kind], to).wait_recv()

    def wait_send(self, kind):
        self.make(kind).wait_send()

    FORWARD = {0: (3,), 1: (4,), 2: (5, 6), 3: (), 4: (), 5: (7,), 6: (8,), 7: (), 8: ()}


def half(ref, part, rows):
    if part == 0:
        return ref
    return ref.at[pl.ds((part - 1) * (rows // 2), rows // 2)]


NAMES = ("query", "key", "value", "d_query", "d_key", "d_value")
STARTS = {"query": 0, "key": 512, "value": 640, "d_query": 768, "d_key": 1280, "d_value": 1408}
WIDTHS = {"query": 512, "key": 128, "value": 128, "d_query": 512, "d_key": 128, "d_value": 128}


def body(
    factor,
    tokens, target, w_query, w_key, w_value, t_query, t_key, t_value, cc, ss, cct, sst,
    out_query, out_key, out_value,
    feat, wbuf, proj, q2, q2t, k2, v2, dk1, dk2, dvt, lowt,
    part, sibr, sums, first, second, pair_out, pair_in, total,
    local_sem, f_send, f_recv, w_send, w_recv, s_send, s_recv, r_send, r_recv,
):
    at = Place()
    sibling = at.fsdp(at.yh, at.z, 1 - at.core)
    up, down = at.along(at.z, 1), at.along(at.z, 3)
    to_up, to_down = at.fsdp(at.yh, up, at.core), at.fsdp(at.yh, down, at.core)
    across = at.fsdp(1 - at.yh, at.z, at.core)

    def f_slot(x, y, piece):
        return half(feat.at[x * 2 + y], piece, T)

    def w_rows(z, yh, core, piece):
        low = pl.multiple_of(core * 256 + (128 if piece == 2 else 0), 128)
        return wbuf.at[yh * 4 + z, pl.ds(low, 256 if piece == 0 else 128)]

    def w_slot(z, yh, piece):
        return w_rows(z, yh, at.core, piece)

    mine = w_slot(at.z, at.yh, 0)
    loads = []
    for number, (name, ref) in enumerate(zip(NAMES, (w_query, w_key, w_value, t_query, t_key, t_value))):
        window = wbuf.at[at.yh * 4 + at.z, pl.ds(pl.multiple_of(at.core * 256, 256), 256), pl.ds(STARTS[name], WIDTHS[name])]
        loads.append(pltpu.make_async_copy(ref, window, local_sem.at[number]))
    loads.append(pltpu.make_async_copy(tokens, f_slot(at.x, at.y, 0), local_sem.at[6]))
    for load in loads:
        load.start()

    ring_f = Ring(at.x, at.y, f_slot, at.tp, tokens, f_send, f_recv)
    ring_w = Ring(at.z, at.yh, w_slot, lambda z, yh: at.fsdp(yh, z, at.core), mine, w_send, w_recv)

    barrier([at.tp(at.along(at.x, 1), at.y), at.tp(at.along(at.x, 3), at.y), at.tp(at.x, 1 - at.y), to_up, to_down, across, sibling])

    for kind in range(3):
        ring_f.start(kind)
    for load in loads[:6]:
        load.wait()
    for kind in range(3):
        ring_w.start(kind)

    def to_sibling(number, chunk, piece):
        src = w_rows(*chunk, at.core, piece)
        return remote(src, src, s_send.at[number], s_recv.at[number], sibling)

    def from_sibling(number, chunk, piece):
        dst = w_rows(*chunk, 1 - at.core, piece)
        return remote(dst, dst, s_send.at[number], s_recv.at[number], sibling)

    shares = [((at.z, at.yh), 0)] + [(kind[3], kind[1]) for kind in ring_w.kinds]
    to_sibling(0, *shares[0]).start()
    for kind in range(9):
        ring_f.wait_recv(kind)
        for other in Ring.FORWARD[kind]:
            ring_f.start(other)
        ring_w.wait_recv(kind)
        for other in Ring.FORWARD[kind]:
            ring_w.start(other)
        to_sibling(kind + 1, *shares[kind + 1]).start()
        if kind == 2:
            proj[...] = jnp.zeros(proj.shape, F32)
            clear(dk1, dk2, dvt)
    loads[6].wait()
    for number in range(10):
        from_sibling(number, *shares[number]).wait_recv()

    def project_part(t, carry):
        for i in range(T // R):
            rows = slice(i * R, (i + 1) * R)
            proj[rows, :] += dot(feat[t, rows, :], wbuf[t])
        return carry

    lax.fori_loop(0, 8, project_part, 0)
    for kind in range(9):
        ring_f.wait_send(kind)
        ring_w.wait_send(kind)
    for number in range(10):
        to_sibling(number, *shares[number]).wait_send()

    def project(name, h, rows):
        if WIDTHS[name] == HD:
            return proj[rows, STARTS[name]:STARTS[name] + HD]
        return proj[rows, pl.ds(pl.multiple_of(STARTS[name] + h * HD, HD), HD)]

    def target_of(h, rows):
        return target[rows, pl.ds(pl.multiple_of(h * HD, HD), HD)]

    prepare(project, cc, ss, q2, q2t, k2, v2)

    keep = pl.ds(pl.multiple_of(at.core * 256, 256), 256)
    give = pl.ds(pl.multiple_of(256 - at.core * 256, 256), 256)
    far = at.along(at.z, 2)

    def swap(b):
        return remote(part.at[b, :, :, give], sibr.at[b], r_send.at[b, 0], r_recv.at[b, 0], sibling)

    def first_up(b):
        return remote(sums.at[b, :, far, pl.ds(0, 64)], first.at[b, 0], r_send.at[b, 1], r_recv.at[b, 1], to_up)

    def first_down(b):
        return remote(sums.at[b, :, far, pl.ds(64, 64)], first.at[b, 1], r_send.at[b, 2], r_recv.at[b, 2], to_down)

    def second_up(b):
        return remote(sums.at[b, :, up], second.at[b, 0], r_send.at[b, 3], r_recv.at[b, 3], to_up)

    def second_down(b):
        return remote(sums.at[b, :, down], second.at[b, 1], r_send.at[b, 4], r_recv.at[b, 4], to_down)

    def third(b):
        return remote(pair_out.at[b], pair_in.at[b], r_send.at[b, 5], r_recv.at[b, 5], across)

    def contract(b, count):
        def one(t, carry):
            for k in range(count):
                part[b + k, t] = dot(lowt[b + k], feat[t]).astype(BF)
            return carry

        lax.fori_loop(0, 8, one, 0)
        for k in range(count):
            swap(b + k).start()

    def stage_one(b):
        swap(b).wait_recv()

        def one(t, carry):
            a, z = t // 4, t % 4
            sums[b, a, z] = (part[b, t, :, keep].astype(F32) + sibr[b, t].astype(F32)).astype(BF)
            return carry

        for t in range(8):
            one(t, 0)
        first_up(b).start()
        first_down(b).start()

    def stage_two(b):
        first_up(b).wait_recv()
        sums[b, :, up, 0:64, :] = (sums[b, :, up, 0:64, :].astype(F32) + first[b, 0].astype(F32)).astype(BF)
        second_up(b).start()
        first_down(b).wait_recv()
        sums[b, :, down, 64:128, :] = (sums[b, :, down, 64:128, :].astype(F32) + first[b, 1].astype(F32)).astype(BF)
        second_down(b).start()

    def stage_three(b):
        second_up(b).wait_recv()
        second_down(b).wait_recv()

        def row(a):
            return sums[b, a, at.z].astype(F32) + second[b, 0, a].astype(F32) + second[b, 1, a].astype(F32)

        pair_out[b] = row(1 - at.yh).astype(BF)
        third(b).start()
        total[b] = row(at.yh)

    def stage_four(b):
        third(b).wait_recv()
        done = (total[b] + pair_in[b].astype(F32)).T
        if b < HEADS:
            out_query[:, b * HD:(b + 1) * HD] = done
        elif b == HEADS:
            out_key[...] = done
        else:
            out_value[...] = done
        for copy in (swap, first_up, first_down, second_up, second_down, third):
            copy(b).wait_send()

    def head(h, carry):
        for i, stage in enumerate((stage_one, stage_two, stage_three)):
            block(h, i, factor, q2, q2t, k2, v2, target_of, cc, ss, dk1, dk2, dvt, lowt)

            @pl.when(h > 0)
            def _():
                stage(h - 1)

        contract(h, 1)
        return carry

    lax.fori_loop(0, HEADS, head, 0)
    finish_key(cct, sst, dk1, dk2, dvt, lowt)
    stage_one(3)
    contract(4, 2)
    stage_two(3)
    stage_one(4)
    stage_one(5)
    stage_three(3)
    stage_two(4)
    stage_two(5)
    stage_three(4)
    stage_three(5)
    for b in range(HEADS + 2):
        stage_four(b)


def shards(tokens, target, w_query, w_key, w_value, t_query, t_key, t_value):
    factor = (T * 16) ** (-0.5)
    cos, sin = rope_tables(T, HD)
    any_space = pl.BlockSpec(memory_space=pl.ANY)
    vmem = pl.BlockSpec(memory_space=pltpu.VMEM)
    dma = pltpu.SemaphoreType.DMA
    return pl.pallas_call(
        functools.partial(body, factor),
        out_shape=(
            jax.ShapeDtypeStruct((256, 512), F32),
            jax.ShapeDtypeStruct((256, 128), F32),
            jax.ShapeDtypeStruct((256, 128), F32),
        ),
        in_specs=[any_space, vmem] + [any_space] * 6 + [vmem] * 4,
        out_specs=(vmem, vmem, vmem),
        scratch_shapes=[
            pltpu.VMEM((8, T, 512), BF),
            pltpu.VMEM((8, 512, COLS), BF),
            pltpu.VMEM((T, COLS), F32),
            pltpu.VMEM((HEADS, T, 256), BF),
            pltpu.VMEM((HEADS, 256, T), BF),
            pltpu.VMEM((T, 256), BF),
            pltpu.VMEM((T, 256), BF),
            pltpu.VMEM((HD, T), F32),
            pltpu.VMEM((HD, T), F32),
            pltpu.VMEM((HD, T), F32),
            pltpu.VMEM((6, HD, T), BF),
            pltpu.VMEM((6, 8, HD, 512), BF),
            pltpu.VMEM((6, 8, HD, 256), BF),
            pltpu.VMEM((6, 2, 4, HD, 256), BF),
            pltpu.VMEM((6, 2, 2, 64, 256), BF),
            pltpu.VMEM((6, 2, 2, HD, 256), BF),
            pltpu.VMEM((6, HD, 256), BF),
            pltpu.VMEM((6, HD, 256), BF),
            pltpu.VMEM((6, HD, 256), F32),
            dma((7,)),
            dma((9,)), dma((9,)),
            dma((9,)), dma((9,)),
            dma((10,)), dma((10,)),
            dma((6, 6)), dma((6, 6)),
        ],
        compiler_params=pltpu.CompilerParams(collective_id=0, has_side_effects=True, vmem_limit_bytes=62 << 20),
        cost_estimate=pl.CostEstimate(flops=25_000_000_000, bytes_accessed=30_000_000, transcendentals=2_000_000),
        name="hvp",
    )(
        tokens, target, w_query, w_key, w_value, t_query, t_key, t_value,
        np.concatenate([cos, cos], axis=1), np.concatenate([-sin, sin], axis=1), cos.T.copy(), sin.T.copy(),
    )


def solution(mesh):
    placed = tuple(P("fsdp", "tp") for _ in range(8))
    return jax.shard_map(
        shards,
        mesh=mesh,
        in_specs=placed,
        out_specs=(P("fsdp", "tp"), P("fsdp", "tp"), P("fsdp", "tp")),
        check_vma=False,
    )
```

```python
import functools
import math

import jax
import jax.numpy as jnp
import numpy as np
from jax import lax
from jax.experimental import pallas as pl
from jax.experimental.pallas import tpu as pltpu
from jax.sharding import PartitionSpec as P

MESH = pl.DeviceIdType.MESH
BF = jnp.bfloat16
F32 = jnp.float32

HD = 128
T = 768
D = 4096
HEADS = 4
R = 256
COLS = 1536
SIGMA = HD ** (-0.5)
LOG2E = 1.4426950408889634


def rope_tables(length, width):
    halfway = width // 2
    frequency = np.exp(np.arange(halfway, dtype=np.float32) * np.float32(-2.0 * math.log(10000.0) / width)).astype(np.float32)
    angles = np.arange(length, dtype=np.float32)[:, None] * frequency[None, :]
    angles = angles.astype(np.float64)
    return np.cos(angles).astype(np.float32), np.sin(angles).astype(np.float32)


def dot(a, b):
    return jnp.dot(a, b, preferred_element_type=F32)


def dot_nt(a, b):
    return lax.dot_general(a, b, (((1,), (1,)), ((), ())), preferred_element_type=F32)


def rope(u, cc, ss):
    return u * cc + pltpu.roll(u, HD // 2, 1) * ss


def unrope(u, cc, ss):
    return u * cc - pltpu.roll(u, HD // 2, 1) * ss


def prepare(project, cc_ref, ss_ref, q2, q2t, k2, v2):
    for i in range(T // R):
        rows = slice(i * R, (i + 1) * R)
        cc, ss = cc_ref[rows, :], ss_ref[rows, :]
        k2[rows, :HD] = rope(project("key", 0, rows), cc, ss).astype(BF)
        k2[rows, HD:] = rope(project("d_key", 0, rows), cc, ss).astype(BF)
        v2[rows, :HD] = project("value", 0, rows).astype(BF)
        v2[rows, HD:] = (project("d_value", 0, rows) * (1.0 / SIGMA)).astype(BF)

    def one(h, carry):
        for i in range(T // R):
            rows = slice(i * R, (i + 1) * R)
            cc, ss = cc_ref[rows, :], ss_ref[rows, :]
            both = jnp.concatenate(
                [
                    rope(project("d_query", h, rows), cc, ss),
                    rope(project("query", h, rows), cc, ss),
                ],
                axis=1,
            )
            q2[h, rows, :] = both.astype(BF)
            q2t[h, :, rows] = both.T.astype(BF)
        return carry

    lax.fori_loop(0, HEADS, one, 0)


def block(h, i, factor, q2, q2t, k2, v2, target, cc_ref, ss_ref, dk1, dk2, dvt, lowt):
    rows = slice(i * R, (i + 1) * R)
    width = (i + 1) * R
    q_both = q2[h, rows, :]
    kr, kd = k2[:width, :HD], k2[:width, HD:]
    vr = v2[:width, :HD]
    s = dot_nt(q_both[:, HD:], kr)
    ds = dot_nt(q_both, k2[:width, :])
    row = lax.broadcasted_iota(jnp.int32, (R, R), 0)
    col = lax.broadcasted_iota(jnp.int32, (R, R), 1)
    last = jnp.where(col <= row, s[:, i * R:], -1e30)
    s = last if i == 0 else jnp.concatenate([s[:, : i * R], last], axis=1)
    top = jnp.max(s, axis=1, keepdims=True)
    e = jnp.exp2((s - top) * (SIGMA * LOG2E))
    p = e * (1.0 / jnp.sum(e, axis=1, keepdims=True))
    w = ds - jnp.sum(p * ds, axis=1, keepdims=True)
    pd = p * w
    pb, pdb = p.astype(BF), pd.astype(BF)
    mixed = dot(pb, v2[:width, :])
    mix = mixed[:, :HD]
    dmix = dot(pdb, vr) + mixed[:, HD:]
    err = (mix - target(h, rows).astype(F32)) * factor
    derr = dmix * factor
    both = jnp.concatenate([derr, err], axis=1)
    both_low = both.astype(BF)
    both_t = both.T.astype(BF)
    dp = dot_nt(both_low[:, HD:], vr)
    ddp = dot_nt(both_low, v2[:width, :])
    delta = jnp.sum(err * mix, axis=1, keepdims=True)
    ddelta = jnp.sum(derr * mix + err * dmix, axis=1, keepdims=True)
    g = dp - delta
    gs = (p * g).astype(BF)
    gd = (p * (w * g + (ddp - ddelta))).astype(BF)
    dq = dot(gd, kr) * (SIGMA * SIGMA) + dot(gs, kd) * SIGMA
    dq = unrope(dq.astype(BF).astype(F32), cc_ref[rows, :], ss_ref[rows, :])
    lowt[h, :, rows] = dq.T.astype(BF)
    dvt[:, :width] += dot(both_t[HD:], pdb) + dot(both_t[:HD], pb)
    dk1[:, :width] += dot(q2t[h, HD:, rows], gd)
    dk2[:, :width] += dot(q2t[h, :HD, rows], gs)


def clear(dk1, dk2, dvt):
    for ref in (dk1, dk2, dvt):
        ref[...] = jnp.zeros(ref.shape, F32)


def finish_key(cct_ref, sst_ref, dk1, dk2, dvt, lowt):
    dk = dk1[...] * (SIGMA * SIGMA) + dk2[...] * SIGMA
    a, b = dk[: HD // 2], dk[HD // 2:]
    ct, st = cct_ref[...], sst_ref[...]
    lowt[HEADS, : HD // 2, :] = (a * ct + b * st).astype(BF)
    lowt[HEADS, HD // 2:, :] = (b * ct - a * st).astype(BF)
    lowt[HEADS + 1] = (dvt[...] * SIGMA).astype(BF)


def barrier(peers):
    sem = pltpu.get_barrier_semaphore()
    for peer in peers:
        pl.semaphore_signal(sem, inc=1, device_id=peer, device_id_type=MESH)
    pl.semaphore_wait(sem, len(peers))


def remote(src, dst, send, recv, peer):
    return pltpu.make_async_remote_copy(
        src_ref=src, dst_ref=dst, send_sem=send, recv_sem=recv, device_id=peer, device_id_type=MESH
    )


class Place:
    def __init__(self):
        self.f = lax.axis_index("fsdp")
        self.t = lax.axis_index("tp")
        self.core = lax.rem(self.f, 2)
        self.z = lax.rem(lax.div(self.f, 2), 4)
        self.yh = lax.div(self.f, 8)
        self.x = lax.div(self.t, 2)
        self.y = lax.rem(self.t, 2)

    def along(self, base, step):
        return lax.rem(base + step, 4)

    def part_peer(self, j):
        yh, z = lax.rem(self.yh + j // 4, 2), lax.rem(self.z + j % 4, 4)
        return self.fsdp(yh, z, self.core), yh * 4 + z

    def fsdp(self, yh, z, core):
        return {"fsdp": (yh * 4 + z) * 2 + core, "tp": self.t}

    def tp(self, x, y):
        return {"fsdp": self.f, "tp": x * 2 + y}


PIECES = 2


class Ring:
    def __init__(self, r, p, slot, peer, own, send, recv):
        self.slot, self.own, self.send, self.recv = slot, own, send, recv
        right, left, far, q = lax.rem(r + 1, 4), lax.rem(r + 3, 4), lax.rem(r + 2, 4), 1 - p
        to_right, to_left, to_pair = peer(right, p), peer(left, p), peer(r, q)
        self.kinds = {}
        forth = list(range(PIECES))
        back = forth[::-1]

        def add(name, chunk, piece, to, arrives):
            self.kinds[name, piece] = (len(self.kinds), chunk, piece, to, arrives)

        for piece in forth:
            add("right", (r, p), piece, to_right, (left, p))
            add("left", (r, p), piece, to_left, (right, p))
            add("pair", (r, p), piece, to_pair, (r, q))
            add("pair_right", (r, q), piece, to_right, (left, q))
            add("pair_left", (r, q), piece, to_left, (right, q))
        self.top, self.bottom = forth[: PIECES // 2], back[: PIECES // 2]
        for piece in self.top:
            add("far_right", (left, p), piece, to_right, (far, p))
            add("pair_far_right", (left, q), piece, to_right, (far, q))
        for piece in self.bottom:
            add("far_left", (right, p), piece, to_left, (far, p))
            add("pair_far_left", (right, q), piece, to_left, (far, q))

    def make(self, key):
        number, chunk, piece, to, _ = self.kinds[key]
        src = self.own(piece) if key[0] in ("right", "left", "pair") else self.slot(*chunk, piece)
        return remote(src, self.slot(*chunk, piece), self.send.at[number], self.recv.at[number], to)

    def start(self, *key):
        self.make(key).start()

    def arrive(self, *key):
        number, _, piece, to, arrives = self.kinds[key]
        ref = self.slot(*arrives, piece)
        remote(ref, ref, self.send.at[number], self.recv.at[number], to).wait_recv()

    def wait_sends(self):
        for key in self.kinds:
            self.make(key).wait_send()


MESSAGES = 7 * PIECES


NAMES = ("query", "key", "value", "d_query", "d_key", "d_value")
STARTS = {"query": 0, "key": 512, "value": 640, "d_query": 768, "d_key": 1280, "d_value": 1408}
WIDTHS = {"query": 512, "key": 128, "value": 128, "d_query": 512, "d_key": 128, "d_value": 128}


def body(
    factor,
    tokens, target_hbm, w_query, w_key, w_value, t_query, t_key, t_value, cc_hbm, ss_hbm, cct_hbm, sst_hbm,
    out_query, out_key, out_value,
    feat, wbuf, proj, q2, q2t, k2, v2, dk1, dk2, dvt, lowt,
    part, sibr, sums, land, target, cc, ss, cct, sst,
    local_sem, f_send, f_recv, w_send, w_recv, s_send, s_recv, r_send, r_recv,
):
    at = Place()
    sibling = at.fsdp(at.yh, at.z, 1 - at.core)
    f_rows, w_rows_of = T // PIECES, 256 // PIECES

    def f_slot(x, y, piece):
        return feat.at[x * 2 + y, pl.ds(piece * f_rows, f_rows)]

    def w_rows(z, yh, core, piece):
        low = pl.multiple_of(core * 256 + piece * w_rows_of, w_rows_of)
        return wbuf.at[yh * 4 + z, pl.ds(low, w_rows_of)]

    def w_slot(z, yh, piece):
        return w_rows(z, yh, at.core, piece)

    loads = []
    for number, (name, ref) in enumerate(zip(NAMES, (w_query, w_key, w_value, t_query, t_key, t_value))):
        window = wbuf.at[at.yh * 4 + at.z, pl.ds(pl.multiple_of(at.core * 256, 256), 256), pl.ds(STARTS[name], WIDTHS[name])]
        loads.append(pltpu.make_async_copy(ref, window, local_sem.at[number]))
    later = [(tokens, feat.at[at.x * 2 + at.y]), (target_hbm, target), (cc_hbm, cc), (ss_hbm, ss), (cct_hbm, cct), (sst_hbm, sst)]
    late = [pltpu.make_async_copy(src, dst, local_sem.at[6 + number]) for number, (src, dst) in enumerate(later)]
    for load in loads + late:
        load.start()

    ring_f = Ring(at.x, at.y, f_slot, at.tp, lambda piece: tokens.at[pl.ds(piece * f_rows, f_rows)], f_send, f_recv)
    ring_w = Ring(at.z, at.yh, w_slot, lambda z, yh: at.fsdp(yh, z, at.core), lambda piece: w_slot(at.z, at.yh, piece), w_send, w_recv)

    peers = [at.tp(at.along(at.x, 1), at.y), at.tp(at.along(at.x, 3), at.y), at.tp(at.x, 1 - at.y), sibling]
    barrier(peers + [at.part_peer(j)[0] for j in range(1, 8)])

    def launch(ring):
        for number in range(PIECES):
            ring.start("right", number)
            ring.start("left", PIECES - 1 - number)
            ring.start("pair", number)

    launch(ring_f)
    for load in loads:
        load.wait()
    launch(ring_w)

    shared = []

    def share(chunk, piece):
        number = len(shared)
        src, dst = w_rows(*chunk, at.core, piece), w_rows(*chunk, 1 - at.core, piece)
        out = remote(src, src, s_send.at[number], s_recv.at[number], sibling)
        out.start()
        shared.append((out, remote(dst, dst, s_send.at[number], s_recv.at[number], sibling)))

    taken = []

    def take():
        for _, incoming in shared[len(taken):]:
            incoming.wait_recv()
            taken.append(incoming)

    def arrive(name, piece, onward=()):
        for ring in (ring_f, ring_w):
            ring.arrive(name, piece)
            for other in onward:
                if (other, piece) in ring.kinds:
                    ring.start(other, piece)
        kind = ring_w.kinds[name, piece]
        share(kind[4], piece)

    for piece in range(PIECES):
        share((at.z, at.yh), piece)
    proj[...] = jnp.zeros(proj.shape, F32)
    clear(dk1, dk2, dvt)
    forth, back = list(range(PIECES)), list(range(PIECES))[::-1]
    for a, b in zip(forth, back):
        arrive("right", a, ("far_right",))
        arrive("left", b, ("far_left",))
    for piece in forth:
        arrive("pair", piece, ("pair_right", "pair_left"))
    for a, b in zip(ring_f.top, ring_f.bottom):
        arrive("far_right", a)
        arrive("far_left", b)
    late[0].wait()
    take()

    def apart(r, p, ring, pair):
        step = lax.rem(r - ring + 4, 4)
        odd = lax.rem(step, 2)
        return lax.rem(p - pair + 2, 2) * (odd + lax.div(step, 2) * (1 - odd) * 2)

    def project_ready(level):
        def one(t, carry):
            away_f = apart(lax.div(t, 2), lax.rem(t, 2), at.x, at.y)
            away_w = apart(lax.rem(t, 4), lax.div(t, 4), at.z, at.yh)

            @pl.when(jnp.maximum(away_f, away_w) == level)
            def _():
                for i in range(T // R):
                    rows = slice(i * R, (i + 1) * R)
                    proj[rows, :] += dot(feat[t, rows, :], wbuf[t])

            return carry

        lax.fori_loop(0, 8, one, 0)

    project_ready(0)
    for a, b in zip(forth, back):
        arrive("pair_right", a, ("pair_far_right",))
        arrive("pair_left", b, ("pair_far_left",))
    take()
    project_ready(1)
    for a, b in zip(ring_f.top, ring_f.bottom):
        arrive("pair_far_right", a)
        arrive("pair_far_left", b)
    take()
    project_ready(2)
    for load in late[1:]:
        load.wait()

    def project(name, h, rows):
        if WIDTHS[name] == HD:
            return proj[rows, STARTS[name]:STARTS[name] + HD]
        return proj[rows, pl.ds(pl.multiple_of(STARTS[name] + h * HD, HD), HD)]

    def target_of(h, rows):
        return target[rows, pl.ds(pl.multiple_of(h * HD, HD), HD)]

    prepare(project, cc, ss, q2, q2t, k2, v2)

    keep = pl.ds(pl.multiple_of(at.core * 256, 256), 256)
    give = pl.ds(pl.multiple_of(256 - at.core * 256, 256), 256)

    def swap(b):
        return remote(part.at[b, :, :, give], sibr.at[b], r_send.at[b, 0], r_recv.at[b, 0], sibling)

    def direct(b, j):
        peer, t = at.part_peer(j)
        return remote(sums.at[b, t], land.at[b, j], r_send.at[b, j], r_recv.at[b, j], peer)

    def contract(b, count):
        def one(t, carry):
            for k in range(count):
                part[b + k, t] = dot(lowt[b + k], feat[t]).astype(BF)
            return carry

        lax.fori_loop(0, 8, one, 0)
        for k in range(count):
            swap(b + k).start()

    def scatter(b):
        swap(b).wait_recv()
        for j in (6, 5, 7, 4, 2, 1, 3, 0):
            t = at.part_peer(j)[1]
            sums[b, t] = (part[b, t, :, keep].astype(F32) + sibr[b, t].astype(F32)).astype(BF)
            if j:
                direct(b, j).start()

    def collect(b):
        done = sums[b, at.yh * 4 + at.z].astype(F32)
        for j in (1, 3, 2, 4, 5, 7, 6):
            direct(b, j).wait_recv()
            done = done + land[b, j].astype(F32)
        done = done.T
        if b < HEADS:
            out_query[:, b * HD:(b + 1) * HD] = done
        elif b == HEADS:
            out_key[...] = done
        else:
            out_value[...] = done

    def head(h, carry):
        for i in range(T // R):
            block(h, i, factor, q2, q2t, k2, v2, target_of, cc, ss, dk1, dk2, dvt, lowt)
            if i == 1:
                pl.when(h > 0)(lambda: scatter(h - 1))
        contract(h, 1)
        return carry

    lax.fori_loop(0, HEADS, head, 0)
    finish_key(cct, sst, dk1, dk2, dvt, lowt)
    scatter(3)
    contract(4, 2)
    collect(0)
    scatter(4)
    scatter(5)
    ring_f.wait_sends()
    ring_w.wait_sends()
    for outgoing, _ in shared:
        outgoing.wait_send()
    for b in range(1, HEADS + 2):
        collect(b)
    for b in range(HEADS + 2):
        swap(b).wait_send()
        for j in range(1, 8):
            direct(b, j).wait_send()


def shards(tokens, target, w_query, w_key, w_value, t_query, t_key, t_value):
    factor = (T * 16) ** (-0.5)
    cos, sin = rope_tables(T, HD)
    any_space = pl.BlockSpec(memory_space=pl.ANY)
    vmem = pl.BlockSpec(memory_space=pltpu.VMEM)
    dma = pltpu.SemaphoreType.DMA
    return pl.pallas_call(
        functools.partial(body, factor),
        out_shape=(
            jax.ShapeDtypeStruct((256, 512), F32),
            jax.ShapeDtypeStruct((256, 128), F32),
            jax.ShapeDtypeStruct((256, 128), F32),
        ),
        in_specs=[any_space] * 12,
        out_specs=(vmem, vmem, vmem),
        scratch_shapes=[
            pltpu.VMEM((8, T, 512), BF),
            pltpu.VMEM((8, 512, COLS), BF),
            pltpu.VMEM((T, COLS), F32),
            pltpu.VMEM((HEADS, T, 256), BF),
            pltpu.VMEM((HEADS, 256, T), BF),
            pltpu.VMEM((T, 256), BF),
            pltpu.VMEM((T, 256), BF),
            pltpu.VMEM((HD, T), F32),
            pltpu.VMEM((HD, T), F32),
            pltpu.VMEM((HD, T), F32),
            pltpu.VMEM((6, HD, T), BF),
            pltpu.VMEM((6, 8, HD, 512), BF),
            pltpu.VMEM((6, 8, HD, 256), BF),
            pltpu.VMEM((6, 8, HD, 256), BF),
            pltpu.VMEM((6, 8, HD, 256), BF),
            pltpu.VMEM((T, 512), BF),
            pltpu.VMEM((T, HD), F32),
            pltpu.VMEM((T, HD), F32),
            pltpu.VMEM((HD // 2, T), F32),
            pltpu.VMEM((HD // 2, T), F32),
            dma((12,)),
            dma((MESSAGES,)), dma((MESSAGES,)),
            dma((MESSAGES,)), dma((MESSAGES,)),
            dma((8 * PIECES,)), dma((8 * PIECES,)),
            dma((6, 8)), dma((6, 8)),
        ],
        compiler_params=pltpu.CompilerParams(collective_id=0, has_side_effects=True, vmem_limit_bytes=62 << 20),
        cost_estimate=pl.CostEstimate(flops=25_000_000_000, bytes_accessed=30_000_000, transcendentals=2_000_000),
        name="hvp",
    )(
        tokens, target, w_query, w_key, w_value, t_query, t_key, t_value,
        np.concatenate([cos, cos], axis=1), np.concatenate([-sin, sin], axis=1), cos.T.copy(), sin.T.copy(),
    )


def solution(mesh):
    placed = tuple(P("fsdp", "tp") for _ in range(8))
    return jax.shard_map(
        shards,
        mesh=mesh,
        in_specs=placed,
        out_specs=(P("fsdp", "tp"), P("fsdp", "tp"), P("fsdp", "tp")),
        check_vma=False,
    )
```

```python
import functools
import math

import jax
import jax.numpy as jnp
import numpy as np
from jax import lax
from jax.experimental import pallas as pl
from jax.experimental.pallas import tpu as pltpu
from jax.sharding import PartitionSpec as P

MESH = pl.DeviceIdType.MESH
BF = jnp.bfloat16
F32 = jnp.float32

HD = 128
T = 768
D = 4096
HEADS = 4
R = 256
COLS = 1536
SIGMA = HD ** (-0.5)
LOG2E = 1.4426950408889634


def rope_tables(length, width):
    halfway = width // 2
    frequency = np.exp(np.arange(halfway, dtype=np.float32) * np.float32(-2.0 * math.log(10000.0) / width)).astype(np.float32)
    angles = np.arange(length, dtype=np.float32)[:, None] * frequency[None, :]
    angles = angles.astype(np.float64)
    return np.cos(angles).astype(np.float32), np.sin(angles).astype(np.float32)


def dot(a, b):
    return jnp.dot(a, b, preferred_element_type=F32)


def dot_nt(a, b):
    return lax.dot_general(a, b, (((1,), (1,)), ((), ())), preferred_element_type=F32)


def rope(u, cc, ss):
    return u * cc + pltpu.roll(u, HD // 2, 1) * ss


def unrope(u, cc, ss):
    return u * cc - pltpu.roll(u, HD // 2, 1) * ss


def prepare(project, cc_ref, ss_ref, q2, q2t, k2, v2):
    for i in range(T // R):
        rows = slice(i * R, (i + 1) * R)
        cc, ss = cc_ref[rows, :], ss_ref[rows, :]
        k2[rows, :HD] = rope(project("key", 0, rows), cc, ss).astype(BF)
        k2[rows, HD:] = rope(project("d_key", 0, rows), cc, ss).astype(BF)
        v2[rows, :HD] = project("value", 0, rows).astype(BF)
        v2[rows, HD:] = (project("d_value", 0, rows) * (1.0 / SIGMA)).astype(BF)

    def one(h, carry):
        for i in range(T // R):
            rows = slice(i * R, (i + 1) * R)
            cc, ss = cc_ref[rows, :], ss_ref[rows, :]
            both = jnp.concatenate(
                [
                    rope(project("d_query", h, rows), cc, ss),
                    rope(project("query", h, rows), cc, ss),
                ],
                axis=1,
            )
            q2[h, rows, :] = both.astype(BF)
            q2t[h, :, rows] = both.T.astype(BF)
        return carry

    lax.fori_loop(0, HEADS, one, 0)


def block_steps(h, i, factor, q2, q2t, k2, v2, target, cc_ref, ss_ref, dk1, dk2, dvt, lowt):
    rows = slice(i * R, (i + 1) * R)
    width = (i + 1) * R
    q_both = q2[h, rows, :]
    kr, kd = k2[:width, :HD], k2[:width, HD:]
    vr = v2[:width, :HD]
    s = dot_nt(q_both[:, HD:], kr)
    ds = dot_nt(q_both, k2[:width, :])
    yield
    row = lax.broadcasted_iota(jnp.int32, (R, R), 0)
    col = lax.broadcasted_iota(jnp.int32, (R, R), 1)
    last = jnp.where(col <= row, s[:, i * R:], -1e30)
    s = last if i == 0 else jnp.concatenate([s[:, : i * R], last], axis=1)
    top = jnp.max(s, axis=1, keepdims=True)
    e = jnp.exp2((s - top) * (SIGMA * LOG2E))
    p = e * (1.0 / jnp.sum(e, axis=1, keepdims=True))
    pb = p.astype(BF)
    mixed = dot(pb, v2[:width, :])
    yield
    w = ds - jnp.sum(p * ds, axis=1, keepdims=True)
    pdb = (p * w).astype(BF)
    dmix = dot(pdb, vr) + mixed[:, HD:]
    mix = mixed[:, :HD]
    yield
    err = (mix - target(h, rows).astype(F32)) * factor
    derr = dmix * factor
    both = jnp.concatenate([derr, err], axis=1)
    both_low = both.astype(BF)
    both_t = both.T.astype(BF)
    dp = dot_nt(both_low[:, HD:], vr)
    ddp = dot_nt(both_low, v2[:width, :])
    yield
    delta = jnp.sum(err * mix, axis=1, keepdims=True)
    ddelta = jnp.sum(derr * mix + err * dmix, axis=1, keepdims=True)
    g = dp - delta
    gs = (p * g).astype(BF)
    gd = (p * (w * g + (ddp - ddelta))).astype(BF)
    dvt[:, :width] += dot(both_t[HD:], pdb) + dot(both_t[:HD], pb)
    yield
    dq = dot(gd, kr) * (SIGMA * SIGMA) + dot(gs, kd) * SIGMA
    dk1[:, :width] += dot(q2t[h, HD:, rows], gd)
    dk2[:, :width] += dot(q2t[h, :HD, rows], gs)
    yield
    dq = unrope(dq.astype(BF).astype(F32), cc_ref[rows, :], ss_ref[rows, :])
    lowt[h, :, rows] = dq.T.astype(BF)


def together(*chains):
    chains = list(chains)
    while chains:
        for chain in list(chains):
            if next(chain, chain) is chain:
                chains.remove(chain)


def chained(*chains):
    for chain in chains:
        yield from chain


def clear(dk1, dk2, dvt):
    for ref in (dk1, dk2, dvt):
        ref[...] = jnp.zeros(ref.shape, F32)


def finish_key(cct_ref, sst_ref, dk1, dk2, dvt, lowt):
    dk = dk1[...] * (SIGMA * SIGMA) + dk2[...] * SIGMA
    a, b = dk[: HD // 2], dk[HD // 2:]
    ct, st = cct_ref[...], sst_ref[...]
    lowt[HEADS, : HD // 2, :] = (a * ct + b * st).astype(BF)
    lowt[HEADS, HD // 2:, :] = (b * ct - a * st).astype(BF)
    lowt[HEADS + 1] = (dvt[...] * SIGMA).astype(BF)


def barrier(peers):
    sem = pltpu.get_barrier_semaphore()
    for peer in peers:
        pl.semaphore_signal(sem, inc=1, device_id=peer, device_id_type=MESH)
    pl.semaphore_wait(sem, len(peers))


def remote(src, dst, send, recv, peer):
    return pltpu.make_async_remote_copy(
        src_ref=src, dst_ref=dst, send_sem=send, recv_sem=recv, device_id=peer, device_id_type=MESH
    )


class Place:
    def __init__(self):
        self.f = lax.axis_index("fsdp")
        self.t = lax.axis_index("tp")
        self.core = lax.rem(self.f, 2)
        self.z = lax.rem(lax.div(self.f, 2), 4)
        self.yh = lax.div(self.f, 8)
        self.x = lax.div(self.t, 2)
        self.y = lax.rem(self.t, 2)

    def along(self, base, step):
        return lax.rem(base + step, 4)

    def part_peer(self, j):
        yh, z = lax.rem(self.yh + j // 4, 2), lax.rem(self.z + j % 4, 4)
        return self.fsdp(yh, z, self.core), yh * 4 + z

    def fsdp(self, yh, z, core):
        return {"fsdp": (yh * 4 + z) * 2 + core, "tp": self.t}

    def tp(self, x, y):
        return {"fsdp": self.f, "tp": x * 2 + y}


PIECES = 2
PAIR_ORDER = (0, 1)
CUT = 80
SCATTER_AT = 3


class Ring:
    def __init__(self, r, p, slot, peer, own, send, recv):
        self.slot, self.own, self.send, self.recv = slot, own, send, recv
        right, left, far, q = lax.rem(r + 1, 4), lax.rem(r + 3, 4), lax.rem(r + 2, 4), 1 - p
        to_right, to_left, to_pair = peer(right, p), peer(left, p), peer(r, q)
        self.kinds = {}
        forth = list(range(PIECES))
        back = forth[::-1]

        def add(name, chunk, piece, to, arrives):
            self.kinds[name, piece] = (len(self.kinds), chunk, piece, to, arrives)

        for piece in forth:
            add("right", (r, p), piece, to_right, (left, p))
            add("left", (r, p), piece, to_left, (right, p))
            add("pair", (r, p), piece, to_pair, (r, q))
            add("pair_right", (r, q), piece, to_right, (left, q))
            add("pair_left", (r, q), piece, to_left, (right, q))
        self.top, self.bottom = forth[: PIECES // 2], back[: PIECES // 2]
        for piece in self.top:
            add("far_right", (left, p), piece, to_right, (far, p))
            add("pair_far_right", (left, q), piece, to_right, (far, q))
        for piece in self.bottom:
            add("far_left", (right, p), piece, to_left, (far, p))
            add("pair_far_left", (right, q), piece, to_left, (far, q))

    def make(self, key):
        number, chunk, piece, to, _ = self.kinds[key]
        src = self.own(piece) if key[0] in ("right", "left", "pair") else self.slot(*chunk, piece)
        return remote(src, self.slot(*chunk, piece), self.send.at[number], self.recv.at[number], to)

    def start(self, *key):
        self.make(key).start()

    def arrive(self, *key):
        number, _, piece, to, arrives = self.kinds[key]
        ref = self.slot(*arrives, piece)
        remote(ref, ref, self.send.at[number], self.recv.at[number], to).wait_recv()

    def wait_sends(self):
        for key in self.kinds:
            self.make(key).wait_send()


MESSAGES = 7 * PIECES


NAMES = ("query", "key", "value", "d_query", "d_key", "d_value")
STARTS = {"query": 0, "key": 512, "value": 640, "d_query": 768, "d_key": 1280, "d_value": 1408}
WIDTHS = {"query": 512, "key": 128, "value": 128, "d_query": 512, "d_key": 128, "d_value": 128}


def body(
    factor,
    tokens, target_hbm, w_query, w_key, w_value, t_query, t_key, t_value, cc_hbm, ss_hbm, cct_hbm, sst_hbm,
    out_query, out_key, out_value,
    feat, wbuf, proj, q2, q2t, k2, v2, dk1, dk2, dvt, lowt,
    part, sibr, sums, land_up, land_step, land_low, land_last, done_low, target, cc, ss, cct, sst,
    local_sem, f_send, f_recv, w_send, w_recv, s_send, s_recv, r_send, r_recv,
):
    at = Place()
    sibling = at.fsdp(at.yh, at.z, 1 - at.core)
    f_rows, w_rows_of = T // PIECES, 256 // PIECES

    def f_slot(x, y, piece):
        return feat.at[x * 2 + y, pl.ds(piece * f_rows, f_rows)]

    def w_rows(z, yh, core, piece):
        low = pl.multiple_of(core * 256 + piece * w_rows_of, w_rows_of)
        return wbuf.at[yh * 4 + z, pl.ds(low, w_rows_of)]

    def w_slot(z, yh, piece):
        return w_rows(z, yh, at.core, piece)

    loads = []
    for number, (name, ref) in enumerate(zip(NAMES, (w_query, w_key, w_value, t_query, t_key, t_value))):
        window = wbuf.at[at.yh * 4 + at.z, pl.ds(pl.multiple_of(at.core * 256, 256), 256), pl.ds(STARTS[name], WIDTHS[name])]
        loads.append(pltpu.make_async_copy(ref, window, local_sem.at[number]))
    later = [(tokens, feat.at[at.x * 2 + at.y]), (target_hbm, target), (cc_hbm, cc), (ss_hbm, ss), (cct_hbm, cct), (sst_hbm, sst)]
    late = [pltpu.make_async_copy(src, dst, local_sem.at[6 + number]) for number, (src, dst) in enumerate(later)]
    for load in loads + late:
        load.start()

    ring_f = Ring(at.x, at.y, f_slot, at.tp, lambda piece: tokens.at[pl.ds(piece * f_rows, f_rows)], f_send, f_recv)
    ring_w = Ring(at.z, at.yh, w_slot, lambda z, yh: at.fsdp(yh, z, at.core), lambda piece: w_slot(at.z, at.yh, piece), w_send, w_recv)

    peers = [at.tp(at.along(at.x, 1), at.y), at.tp(at.along(at.x, 3), at.y), at.tp(at.x, 1 - at.y), sibling]
    barrier(peers + [at.part_peer(j)[0] for j in (1, 2, 3, 4)])

    def launch(ring):
        for number in range(PIECES):
            ring.start("right", number)
            ring.start("left", PIECES - 1 - number)
            ring.start("pair", PAIR_ORDER[number])

    launch(ring_f)
    for load in loads:
        load.wait()
    launch(ring_w)

    shared = []

    def share(chunk, piece):
        number = len(shared)
        src, dst = w_rows(*chunk, at.core, piece), w_rows(*chunk, 1 - at.core, piece)
        out = remote(src, src, s_send.at[number], s_recv.at[number], sibling)
        out.start()
        shared.append((out, remote(dst, dst, s_send.at[number], s_recv.at[number], sibling)))

    taken = []

    def take():
        for _, incoming in shared[len(taken):]:
            incoming.wait_recv()
            taken.append(incoming)

    def arrive(name, piece, onward=()):
        for ring in (ring_f, ring_w):
            ring.arrive(name, piece)
            for other in onward:
                if (other, piece) in ring.kinds:
                    ring.start(other, piece)
        kind = ring_w.kinds[name, piece]
        share(kind[4], piece)

    for piece in range(PIECES):
        share((at.z, at.yh), piece)
    proj[...] = jnp.zeros(proj.shape, F32)
    clear(dk1, dk2, dvt)
    forth, back = list(range(PIECES)), list(range(PIECES))[::-1]
    for a, b in zip(forth, back):
        arrive("right", a, ("far_right",))
        arrive("left", b, ("far_left",))
    for piece in forth:
        arrive("pair", piece, ("pair_right", "pair_left"))
    for a, b in zip(ring_f.top, ring_f.bottom):
        arrive("far_right", a)
        arrive("far_left", b)
    late[0].wait()
    take()

    def apart(r, p, ring, pair):
        step = lax.rem(r - ring + 4, 4)
        odd = lax.rem(step, 2)
        return lax.rem(p - pair + 2, 2) * (odd + lax.div(step, 2) * (1 - odd) * 2)

    def project_ready(level):
        def one(t, carry):
            away_f = apart(lax.div(t, 2), lax.rem(t, 2), at.x, at.y)
            away_w = apart(lax.rem(t, 4), lax.div(t, 4), at.z, at.yh)

            @pl.when(jnp.maximum(away_f, away_w) == level)
            def _():
                for i in range(T // R):
                    rows = slice(i * R, (i + 1) * R)
                    proj[rows, :] += dot(feat[t, rows, :], wbuf[t])

            return carry

        lax.fori_loop(0, 8, one, 0)

    project_ready(0)
    for a, b in zip(forth, back):
        arrive("pair_right", a, ("pair_far_right",))
        arrive("pair_left", b, ("pair_far_left",))
    take()
    project_ready(1)
    for a, b in zip(ring_f.top, ring_f.bottom):
        arrive("pair_far_right", a)
        arrive("pair_far_left", b)
    take()
    project_ready(2)
    for load in late[1:]:
        load.wait()

    def project(name, h, rows):
        if WIDTHS[name] == HD:
            return proj[rows, STARTS[name]:STARTS[name] + HD]
        return proj[rows, pl.ds(pl.multiple_of(STARTS[name] + h * HD, HD), HD)]

    def target_of(h, rows):
        return target[rows, pl.ds(pl.multiple_of(h * HD, HD), HD)]

    prepare(project, cc, ss, q2, q2t, k2, v2)

    keep = pl.ds(pl.multiple_of(at.core * 256, 256), 256)
    give = pl.ds(pl.multiple_of(256 - at.core * 256, 256), 256)

    over = 1 - at.yh
    upper, lower = pl.ds(0, CUT), pl.ds(CUT, HD - CUT)
    across = at.part_peer(4)[0]
    steps = [(j, at.along(at.z, j), at.part_peer(j)[0]) for j in (2, 1, 3)]

    def push(b, number, src, dst, peer):
        return remote(src, dst, r_send.at[b, number], r_recv.at[b, number], peer)

    def swap(b):
        return push(b, 0, part.at[lax.rem(b, 3), :, :, :, give], sibr.at[b], sibling)

    def upper_pair(b):
        return push(b, 1, sums.at[b, over, :, upper], land_up.at[b], across)

    def upper_step(b, j, z, peer):
        return push(b, 1 + j, sums.at[b, at.yh, z, upper], land_step.at[b, j], peer)

    def lower_step(b, j, z, peer):
        return push(b, 4 + j, sums.at[b, :, z, lower], land_low.at[b, j], peer)

    def lower_pair(b):
        return push(b, 8, sums.at[b, over, at.z, lower], land_last.at[b], across)

    def contract(b, count):
        def one(t, carry):
            low = lowt[pl.ds(b, count)].reshape(count * HD, T)
            both = dot(low, feat[t]).astype(BF)
            for k in range(count):
                part[lax.rem(b + k, 3), t // 4, t % 4] = both[k * HD:(k + 1) * HD]
            return carry

        lax.fori_loop(0, 8, one, 0)
        for k in range(count):
            swap(b + k).start()

    def add_halves(b, yh, z, rows):
        sums[b, yh, z, rows] = (
            part[lax.rem(b, 3), yh, z, rows, keep].astype(F32) + sibr[b, yh, z, rows].astype(F32)
        ).astype(BF)

    def scatter(b):
        swap(b).wait_recv()
        for z in range(4):
            add_halves(b, over, z, upper)
        upper_pair(b).start()
        for step in steps:
            for yh in range(2):
                add_halves(b, yh, step[1], lower)
            lower_step(b, *step).start()
        for z in range(4):
            add_halves(b, at.yh, z, upper)
        for yh in range(2):
            add_halves(b, yh, at.z, lower)

    def relay(b):
        upper_pair(b).wait_recv()
        for step in steps:
            z = step[1]
            sums[b, at.yh, z, upper] = (sums[b, at.yh, z, upper].astype(F32) + land_up[b, z].astype(F32)).astype(BF)
            upper_step(b, *step).start()
        for step in steps:
            lower_step(b, *step).wait_recv()

        def total(yh):
            return (
                sums[b, yh, at.z, lower].astype(F32) + land_low[b, 1, yh].astype(F32)
                + land_low[b, 2, yh].astype(F32) + land_low[b, 3, yh].astype(F32)
            )

        sums[b, over, at.z, lower] = total(over).astype(BF)
        lower_pair(b).start()
        done_low[b] = total(at.yh)

    def collect(b):
        done = sums[b, at.yh, at.z, upper].astype(F32) + land_up[b, at.z].astype(F32)
        for step in steps:
            upper_step(b, *step).wait_recv()
            done = done + land_step[b, step[0]].astype(F32)
        lower_pair(b).wait_recv()
        done = jnp.concatenate([done, done_low[b] + land_last[b].astype(F32)], axis=0).T
        if b < HEADS:
            out_query[:, b * HD:(b + 1) * HD] = done
        elif b == HEADS:
            out_key[...] = done
        else:
            out_value[...] = done

    def attend(h, *others):
        together(
            *[
                block_steps(h, i, factor, q2, q2t, k2, v2, target_of, cc, ss, dk1, dk2, dvt, lowt)
                for i in range(T // R - 1, -1, -1)
            ],
            *others,
        )

    def scatter_inside(b):
        for _ in range(SCATTER_AT):
            yield
        scatter(b)

    def head(h, carry):
        attend(h, scatter_inside(h - 1))
        pl.when(h > 1)(lambda: relay(h - 2))
        pl.when(h == 3)(lambda: swap(0).wait_send())
        contract(h, 1)
        return carry

    attend(0)
    contract(0, 1)
    lax.fori_loop(1, HEADS, head, 0)
    finish_key(cct, sst, dk1, dk2, dvt, lowt)
    relay(2)
    scatter(3)
    swap(1).wait_send()
    swap(2).wait_send()
    contract(4, 2)
    scatter(4)
    scatter(5)
    relay(3)
    ring_f.wait_sends()
    ring_w.wait_sends()
    for outgoing, _ in shared:
        outgoing.wait_send()
    for b in range(3):
        collect(b)
    relay(4)
    relay(5)
    for b in range(3, HEADS + 2):
        collect(b)
    for b in range(HEADS + 2):
        if b > 2:
            swap(b).wait_send()
        upper_pair(b).wait_send()
        lower_pair(b).wait_send()
        for step in steps:
            upper_step(b, *step).wait_send()
            lower_step(b, *step).wait_send()


def shards(tokens, target, w_query, w_key, w_value, t_query, t_key, t_value):
    factor = (T * 16) ** (-0.5)
    cos, sin = rope_tables(T, HD)
    any_space = pl.BlockSpec(memory_space=pl.ANY)
    vmem = pl.BlockSpec(memory_space=pltpu.VMEM)
    dma = pltpu.SemaphoreType.DMA
    return pl.pallas_call(
        functools.partial(body, factor),
        out_shape=(
            jax.ShapeDtypeStruct((256, 512), F32),
            jax.ShapeDtypeStruct((256, 128), F32),
            jax.ShapeDtypeStruct((256, 128), F32),
        ),
        in_specs=[any_space] * 12,
        out_specs=(vmem, vmem, vmem),
        scratch_shapes=[
            pltpu.VMEM((8, T, 512), BF),
            pltpu.VMEM((8, 512, COLS), BF),
            pltpu.VMEM((T, COLS), F32),
            pltpu.VMEM((HEADS, T, 256), BF),
            pltpu.VMEM((HEADS, 256, T), BF),
            pltpu.VMEM((T, 256), BF),
            pltpu.VMEM((T, 256), BF),
            pltpu.VMEM((HD, T), F32),
            pltpu.VMEM((HD, T), F32),
            pltpu.VMEM((HD, T), F32),
            pltpu.VMEM((6, HD, T), BF),
            pltpu.VMEM((3, 2, 4, HD, 512), BF),
            pltpu.VMEM((6, 2, 4, HD, 256), BF),
            pltpu.VMEM((6, 2, 4, HD, 256), BF),
            pltpu.VMEM((6, 4, CUT, 256), BF),
            pltpu.VMEM((6, 4, CUT, 256), BF),
            pltpu.VMEM((6, 4, 2, HD - CUT, 256), BF),
            pltpu.VMEM((6, HD - CUT, 256), BF),
            pltpu.VMEM((6, HD - CUT, 256), F32),
            pltpu.VMEM((T, 512), BF),
            pltpu.VMEM((T, HD), F32),
            pltpu.VMEM((T, HD), F32),
            pltpu.VMEM((HD // 2, T), F32),
            pltpu.VMEM((HD // 2, T), F32),
            dma((12,)),
            dma((MESSAGES,)), dma((MESSAGES,)),
            dma((MESSAGES,)), dma((MESSAGES,)),
            dma((8 * PIECES,)), dma((8 * PIECES,)),
            dma((6, 9)), dma((6, 9)),
        ],
        compiler_params=pltpu.CompilerParams(collective_id=0, has_side_effects=True, vmem_limit_bytes=62 << 20),
        cost_estimate=pl.CostEstimate(flops=25_000_000_000, bytes_accessed=30_000_000, transcendentals=2_000_000),
        name="hvp",
    )(
        tokens, target, w_query, w_key, w_value, t_query, t_key, t_value,
        np.concatenate([cos, cos], axis=1), np.concatenate([-sin, sin], axis=1), cos.T.copy(), sin.T.copy(),
    )


def solution(mesh):
    placed = tuple(P("fsdp", "tp") for _ in range(8))
    return jax.shard_map(
        shards,
        mesh=mesh,
        in_specs=placed,
        out_specs=(P("fsdp", "tp"), P("fsdp", "tp"), P("fsdp", "tp")),
        check_vma=False,
    )
```

```python
import functools
import math

import jax
import jax.numpy as jnp
import numpy as np
from jax import lax
from jax.experimental import pallas as pl
from jax.experimental.pallas import tpu as pltpu
from jax.sharding import PartitionSpec as P

MESH = pl.DeviceIdType.MESH
BF = jnp.bfloat16
F32 = jnp.float32

HD = 128
T = 768
D = 4096
HEADS = 4
R = 256
COLS = 1536
SIGMA = HD ** (-0.5)
LOG2E = 1.4426950408889634


def rope_tables(length, width):
    halfway = width // 2
    frequency = np.exp(np.arange(halfway, dtype=np.float32) * np.float32(-2.0 * math.log(10000.0) / width)).astype(np.float32)
    angles = np.arange(length, dtype=np.float32)[:, None] * frequency[None, :]
    angles = angles.astype(np.float64)
    return np.cos(angles).astype(np.float32), np.sin(angles).astype(np.float32)


def dot(a, b):
    return jnp.dot(a, b, preferred_element_type=F32)


def dot_nt(a, b):
    return lax.dot_general(a, b, (((1,), (1,)), ((), ())), preferred_element_type=F32)


def rope(u, cc, ss):
    return u * cc + pltpu.roll(u, HD // 2, 1) * ss


def unrope(u, cc, ss):
    return u * cc - pltpu.roll(u, HD // 2, 1) * ss


def prepare(project, cc_ref, ss_ref, q2, q2t, k2, v2):
    for i in range(T // R):
        rows = slice(i * R, (i + 1) * R)
        cc, ss = cc_ref[rows, :], ss_ref[rows, :]
        k2[rows, :HD] = rope(project("key", 0, rows), cc, ss).astype(BF)
        k2[rows, HD:] = rope(project("d_key", 0, rows), cc, ss).astype(BF)
        v2[rows, :HD] = project("value", 0, rows).astype(BF)
        v2[rows, HD:] = (project("d_value", 0, rows) * (1.0 / SIGMA)).astype(BF)

    def one(h, carry):
        for i in range(T // R):
            rows = slice(i * R, (i + 1) * R)
            cc, ss = cc_ref[rows, :], ss_ref[rows, :]
            both = jnp.concatenate(
                [
                    rope(project("d_query", h, rows), cc, ss),
                    rope(project("query", h, rows), cc, ss),
                ],
                axis=1,
            )
            q2[h, rows, :] = both.astype(BF)
            q2t[h, :, rows] = both.T.astype(BF)
        return carry

    lax.fori_loop(0, HEADS, one, 0)


def block_steps(h, i, factor, q2, q2t, k2, v2, target, cc_ref, ss_ref, dk1, dk2, dvt, lowt):
    rows = slice(i * R, (i + 1) * R)
    width = (i + 1) * R
    q_both = q2[h, rows, :]
    kr, kd = k2[:width, :HD], k2[:width, HD:]
    vr = v2[:width, :HD]
    s = dot_nt(q_both[:, HD:], kr)
    ds = dot_nt(q_both, k2[:width, :])
    yield
    row = lax.broadcasted_iota(jnp.int32, (R, R), 0)
    col = lax.broadcasted_iota(jnp.int32, (R, R), 1)
    last = jnp.where(col <= row, s[:, i * R:], -1e30)
    s = last if i == 0 else jnp.concatenate([s[:, : i * R], last], axis=1)
    top = jnp.max(s, axis=1, keepdims=True)
    e = jnp.exp2((s - top) * (SIGMA * LOG2E))
    p = e * (1.0 / jnp.sum(e, axis=1, keepdims=True))
    pb = p.astype(BF)
    mixed = dot(pb, v2[:width, :])
    yield
    w = ds - jnp.sum(p * ds, axis=1, keepdims=True)
    pdb = (p * w).astype(BF)
    dmix = dot(pdb, vr) + mixed[:, HD:]
    mix = mixed[:, :HD]
    yield
    err = (mix - target(h, rows).astype(F32)) * factor
    derr = dmix * factor
    both = jnp.concatenate([derr, err], axis=1)
    both_low = both.astype(BF)
    both_t = both.T.astype(BF)
    dp = dot_nt(both_low[:, HD:], vr)
    ddp = dot_nt(both_low, v2[:width, :])
    yield
    delta = jnp.sum(err * mix, axis=1, keepdims=True)
    ddelta = jnp.sum(derr * mix + err * dmix, axis=1, keepdims=True)
    g = dp - delta
    gs = (p * g).astype(BF)
    gd = (p * (w * g + (ddp - ddelta))).astype(BF)
    dvt[:, :width] += dot(both_t[HD:], pdb) + dot(both_t[:HD], pb)
    yield
    dq = dot(gd, kr) * (SIGMA * SIGMA) + dot(gs, kd) * SIGMA
    dk1[:, :width] += dot(q2t[h, HD:, rows], gd)
    dk2[:, :width] += dot(q2t[h, :HD, rows], gs)
    yield
    dq = unrope(dq.astype(BF).astype(F32), cc_ref[rows, :], ss_ref[rows, :])
    lowt[h, :, rows] = dq.T.astype(BF)


def together(*chains):
    chains = list(chains)
    while chains:
        for chain in list(chains):
            if next(chain, chain) is chain:
                chains.remove(chain)


def chained(*chains):
    for chain in chains:
        yield from chain


def clear(dk1, dk2, dvt):
    for ref in (dk1, dk2, dvt):
        ref[...] = jnp.zeros(ref.shape, F32)


def finish_key(cct_ref, sst_ref, dk1, dk2, dvt, lowt):
    dk = dk1[...] * (SIGMA * SIGMA) + dk2[...] * SIGMA
    a, b = dk[: HD // 2], dk[HD // 2:]
    ct, st = cct_ref[...], sst_ref[...]
    lowt[HEADS, : HD // 2, :] = (a * ct + b * st).astype(BF)
    lowt[HEADS, HD // 2:, :] = (b * ct - a * st).astype(BF)
    lowt[HEADS + 1] = (dvt[...] * SIGMA).astype(BF)


def barrier(peers):
    sem = pltpu.get_barrier_semaphore()
    for peer in peers:
        pl.semaphore_signal(sem, inc=1, device_id=peer, device_id_type=MESH)
    pl.semaphore_wait(sem, len(peers))


def remote(src, dst, send, recv, peer):
    return pltpu.make_async_remote_copy(
        src_ref=src, dst_ref=dst, send_sem=send, recv_sem=recv, device_id=peer, device_id_type=MESH
    )


class Place:
    def __init__(self):
        self.f = lax.axis_index("fsdp")
        self.t = lax.axis_index("tp")
        self.core = lax.rem(self.f, 2)
        self.z = lax.rem(lax.div(self.f, 2), 4)
        self.yh = lax.div(self.f, 8)
        self.x = lax.div(self.t, 2)
        self.y = lax.rem(self.t, 2)

    def along(self, base, step):
        return lax.rem(base + step, 4)

    def part_peer(self, j):
        yh, z = lax.rem(self.yh + j // 4, 2), lax.rem(self.z + j % 4, 4)
        return self.fsdp(yh, z, self.core), yh * 4 + z

    def fsdp(self, yh, z, core):
        return {"fsdp": (yh * 4 + z) * 2 + core, "tp": self.t}

    def tp(self, x, y):
        return {"fsdp": self.f, "tp": x * 2 + y}


PIECES = 2
PAIR_ORDER = (0, 1)
CUT = 80
SCATTER_AT = 3


class Ring:
    def __init__(self, r, p, slot, peer, own, send, recv):
        self.slot, self.own, self.send, self.recv = slot, own, send, recv
        right, left, far, q = lax.rem(r + 1, 4), lax.rem(r + 3, 4), lax.rem(r + 2, 4), 1 - p
        to_right, to_left, to_pair = peer(right, p), peer(left, p), peer(r, q)
        self.kinds = {}
        forth = list(range(PIECES))
        back = forth[::-1]

        def add(name, chunk, piece, to, arrives):
            self.kinds[name, piece] = (len(self.kinds), chunk, piece, to, arrives)

        for piece in forth:
            add("right", (r, p), piece, to_right, (left, p))
            add("left", (r, p), piece, to_left, (right, p))
            add("pair", (r, p), piece, to_pair, (r, q))
            add("pair_right", (r, q), piece, to_right, (left, q))
            add("pair_left", (r, q), piece, to_left, (right, q))
        self.top, self.bottom = forth[: PIECES // 2], back[: PIECES // 2]
        for piece in self.top:
            add("far_right", (left, p), piece, to_right, (far, p))
            add("pair_far_right", (left, q), piece, to_right, (far, q))
        for piece in self.bottom:
            add("far_left", (right, p), piece, to_left, (far, p))
            add("pair_far_left", (right, q), piece, to_left, (far, q))

    def make(self, key):
        number, chunk, piece, to, _ = self.kinds[key]
        src = self.own(piece) if key[0] in ("right", "left", "pair") else self.slot(*chunk, piece)
        return remote(src, self.slot(*chunk, piece), self.send.at[number], self.recv.at[number], to)

    def start(self, *key):
        self.make(key).start()

    def arrive(self, *key):
        number, _, piece, to, arrives = self.kinds[key]
        ref = self.slot(*arrives, piece)
        remote(ref, ref, self.send.at[number], self.recv.at[number], to).wait_recv()

    def wait_sends(self):
        for key in self.kinds:
            self.make(key).wait_send()


MESSAGES = 7 * PIECES


NAMES = ("query", "key", "value", "d_query", "d_key", "d_value")
STARTS = {"query": 0, "key": 512, "value": 640, "d_query": 768, "d_key": 1280, "d_value": 1408}
WIDTHS = {"query": 512, "key": 128, "value": 128, "d_query": 512, "d_key": 128, "d_value": 128}


def body(
    factor,
    tokens, target_hbm, w_query, w_key, w_value, t_query, t_key, t_value, cc_hbm, ss_hbm, cct_hbm, sst_hbm,
    out_query, out_key, out_value,
    feat, wbuf, proj, q2, q2t, k2, v2, dk1, dk2, dvt, lowt,
    part, sibr, sums, land_up, land_step, land_low, land_last, done_low, target, cc, ss, cct, sst,
    local_sem, f_send, f_recv, w_send, w_recv, s_send, s_recv, r_send, r_recv,
):
    at = Place()
    sibling = at.fsdp(at.yh, at.z, 1 - at.core)
    f_rows, w_rows_of = T // PIECES, 256 // PIECES

    def f_slot(x, y, piece):
        return feat.at[x * 2 + y, pl.ds(piece * f_rows, f_rows)]

    def w_rows(z, yh, core, piece):
        low = pl.multiple_of(core * 256 + piece * w_rows_of, w_rows_of)
        return wbuf.at[yh * 4 + z, pl.ds(low, w_rows_of)]

    def w_slot(z, yh, piece):
        return w_rows(z, yh, at.core, piece)

    loads = []
    for number, (name, ref) in enumerate(zip(NAMES, (w_query, w_key, w_value, t_query, t_key, t_value))):
        window = wbuf.at[at.yh * 4 + at.z, pl.ds(pl.multiple_of(at.core * 256, 256), 256), pl.ds(STARTS[name], WIDTHS[name])]
        loads.append(pltpu.make_async_copy(ref, window, local_sem.at[number]))
    later = [(tokens, feat.at[at.x * 2 + at.y]), (target_hbm, target), (cc_hbm, cc), (ss_hbm, ss), (cct_hbm, cct), (sst_hbm, sst)]
    late = [pltpu.make_async_copy(src, dst, local_sem.at[6 + number]) for number, (src, dst) in enumerate(later)]
    for load in loads + late:
        load.start()

    ring_f = Ring(at.x, at.y, f_slot, at.tp, lambda piece: tokens.at[pl.ds(piece * f_rows, f_rows)], f_send, f_recv)
    ring_w = Ring(at.z, at.yh, w_slot, lambda z, yh: at.fsdp(yh, z, at.core), lambda piece: w_slot(at.z, at.yh, piece), w_send, w_recv)

    peers = [at.tp(at.along(at.x, 1), at.y), at.tp(at.along(at.x, 3), at.y), at.tp(at.x, 1 - at.y), sibling]
    barrier(peers + [at.part_peer(j)[0] for j in (1, 2, 3, 4)])

    def launch(ring):
        for number in range(PIECES):
            ring.start("right", number)
            ring.start("left", PIECES - 1 - number)
            ring.start("pair", PAIR_ORDER[number])

    launch(ring_f)
    for load in loads:
        load.wait()
    launch(ring_w)

    shared = []

    def share(chunk, piece):
        number = len(shared)
        src, dst = w_rows(*chunk, at.core, piece), w_rows(*chunk, 1 - at.core, piece)
        out = remote(src, src, s_send.at[number], s_recv.at[number], sibling)
        out.start()
        shared.append((out, remote(dst, dst, s_send.at[number], s_recv.at[number], sibling)))

    taken = []

    def take():
        for _, incoming in shared[len(taken):]:
            incoming.wait_recv()
            taken.append(incoming)

    def arrive(name, piece, onward=()):
        for ring in (ring_f, ring_w):
            ring.arrive(name, piece)
            for other in onward:
                if (other, piece) in ring.kinds:
                    ring.start(other, piece)
        kind = ring_w.kinds[name, piece]
        share(kind[4], piece)

    for piece in range(PIECES):
        share((at.z, at.yh), piece)
    proj[...] = jnp.zeros(proj.shape, F32)
    clear(dk1, dk2, dvt)
    forth, back = list(range(PIECES)), list(range(PIECES))[::-1]
    for a, b in zip(forth, back):
        arrive("right", a, ("far_right",))
        arrive("left", b, ("far_left",))
    for piece in forth:
        arrive("pair", piece, ("pair_right", "pair_left"))
    for a, b in zip(ring_f.top, ring_f.bottom):
        arrive("far_right", a)
        arrive("far_left", b)
    late[0].wait()
    take()

    def apart(r, p, ring, pair):
        step = lax.rem(r - ring + 4, 4)
        odd = lax.rem(step, 2)
        return lax.rem(p - pair + 2, 2) * (odd + lax.div(step, 2) * (1 - odd) * 2)

    def project_ready(level):
        def one(t, carry):
            away_f = apart(lax.div(t, 2), lax.rem(t, 2), at.x, at.y)
            away_w = apart(lax.rem(t, 4), lax.div(t, 4), at.z, at.yh)

            @pl.when(jnp.maximum(away_f, away_w) == level)
            def _():
                for i in range(T // R):
                    rows = slice(i * R, (i + 1) * R)
                    proj[rows, :] += dot(feat[t, rows, :], wbuf[t])

            return carry

        lax.fori_loop(0, 8, one, 0)

    project_ready(0)
    for a, b in zip(forth, back):
        arrive("pair_right", a, ("pair_far_right",))
        arrive("pair_left", b, ("pair_far_left",))
    take()
    project_ready(1)
    for a, b in zip(ring_f.top, ring_f.bottom):
        arrive("pair_far_right", a)
        arrive("pair_far_left", b)
    take()
    project_ready(2)
    for load in late[1:]:
        load.wait()

    def project(name, h, rows):
        if WIDTHS[name] == HD:
            return proj[rows, STARTS[name]:STARTS[name] + HD]
        return proj[rows, pl.ds(pl.multiple_of(STARTS[name] + h * HD, HD), HD)]

    def target_of(h, rows):
        return target[rows, pl.ds(pl.multiple_of(h * HD, HD), HD)]

    prepare(project, cc, ss, q2, q2t, k2, v2)

    keep = pl.ds(pl.multiple_of(at.core * 256, 256), 256)
    give = pl.ds(pl.multiple_of(256 - at.core * 256, 256), 256)

    over = 1 - at.yh
    upper, lower = pl.ds(0, CUT), pl.ds(CUT, HD - CUT)
    across = at.part_peer(4)[0]
    steps = [(j, at.along(at.z, j), at.part_peer(j)[0]) for j in (2, 1, 3)]

    def push(b, number, src, dst, peer):
        return remote(src, dst, r_send.at[b, number], r_recv.at[b, number], peer)

    def swap(b):
        return push(b, 0, part.at[lax.rem(b, 3), :, :, :, give], sibr.at[b], sibling)

    def upper_pair(b):
        return push(b, 1, sums.at[b, over, :, upper], land_up.at[b], across)

    def upper_step(b, j, z, peer):
        return push(b, 1 + j, sums.at[b, at.yh, z, upper], land_step.at[b, j], peer)

    def lower_step(b, j, z, peer):
        return push(b, 4 + j, sums.at[b, :, z, lower], land_low.at[b, j], peer)

    def lower_pair(b):
        return push(b, 8, sums.at[b, over, at.z, lower], land_last.at[b], across)

    def contract(b, count):
        def one(t, carry):
            low = lowt[pl.ds(b, count)].reshape(count * HD, T)
            both = dot(low, feat[t]).astype(BF)
            for k in range(count):
                part[lax.rem(b + k, 3), t // 4, t % 4] = both[k * HD:(k + 1) * HD]
            return carry

        lax.fori_loop(0, 8, one, 0)
        for k in range(count):
            swap(b + k).start()

    def add_halves(b, yh, z, rows):
        sums[b, yh, z, rows] = (
            part[lax.rem(b, 3), yh, z, rows, keep].astype(F32) + sibr[b, yh, z, rows].astype(F32)
        ).astype(BF)

    def scatter(b):
        swap(b).wait_recv()
        for z in range(4):
            add_halves(b, over, z, upper)
        upper_pair(b).start()
        for step in steps:
            for yh in range(2):
                add_halves(b, yh, step[1], lower)
            lower_step(b, *step).start()
        for z in range(4):
            add_halves(b, at.yh, z, upper)
        for yh in range(2):
            add_halves(b, yh, at.z, lower)

    def relay(b):
        upper_pair(b).wait_recv()
        for step in steps:
            z = step[1]
            sums[b, at.yh, z, upper] = (sums[b, at.yh, z, upper].astype(F32) + land_up[b, z].astype(F32)).astype(BF)
            upper_step(b, *step).start()
        for step in steps:
            lower_step(b, *step).wait_recv()

        def total(yh):
            return (
                sums[b, yh, at.z, lower].astype(F32) + land_low[b, 1, yh].astype(F32)
                + land_low[b, 2, yh].astype(F32) + land_low[b, 3, yh].astype(F32)
            )

        sums[b, over, at.z, lower] = total(over).astype(BF)
        lower_pair(b).start()
        done_low[b] = total(at.yh)

    def collect(b):
        done = sums[b, at.yh, at.z, upper].astype(F32) + land_up[b, at.z].astype(F32)
        for step in steps:
            upper_step(b, *step).wait_recv()
            done = done + land_step[b, step[0]].astype(F32)
        lower_pair(b).wait_recv()
        done = jnp.concatenate([done, done_low[b] + land_last[b].astype(F32)], axis=0).T
        if b < HEADS:
            out_query[:, b * HD:(b + 1) * HD] = done
        elif b == HEADS:
            out_key[...] = done
        else:
            out_value[...] = done

    def attend(h, *others):
        together(
            *[
                block_steps(h, i, factor, q2, q2t, k2, v2, target_of, cc, ss, dk1, dk2, dvt, lowt)
                for i in range(T // R - 1, -1, -1)
            ],
            *others,
        )

    def scatter_inside(b):
        for _ in range(SCATTER_AT):
            yield
        scatter(b)

    def contract_inside(b):
        low = lowt[b]
        for t in range(8):
            part[b % 3, t // 4, t % 4] = dot(low, feat[t]).astype(BF)
            yield

    attend(0)
    attend(1, contract_inside(0))
    swap(0).start()
    attend(2, contract_inside(1), scatter_inside(0))
    swap(1).start()
    attend(3, contract_inside(2), scatter_inside(1))
    swap(2).start()
    finish_key(cct, sst, dk1, dk2, dvt, lowt)
    relay(0)
    scatter(2)
    for b in range(3):
        swap(b).wait_send()
    contract(3, 3)
    relay(1)
    scatter(3)
    scatter(4)
    scatter(5)
    relay(2)
    ring_f.wait_sends()
    ring_w.wait_sends()
    for outgoing, _ in shared:
        outgoing.wait_send()
    collect(0)
    collect(1)
    relay(3)
    relay(4)
    relay(5)
    for b in range(2, HEADS + 2):
        collect(b)
    for b in range(HEADS + 2):
        if b > 2:
            swap(b).wait_send()
        upper_pair(b).wait_send()
        lower_pair(b).wait_send()
        for step in steps:
            upper_step(b, *step).wait_send()
            lower_step(b, *step).wait_send()


def shards(tokens, target, w_query, w_key, w_value, t_query, t_key, t_value):
    factor = (T * 16) ** (-0.5)
    cos, sin = rope_tables(T, HD)
    any_space = pl.BlockSpec(memory_space=pl.ANY)
    vmem = pl.BlockSpec(memory_space=pltpu.VMEM)
    dma = pltpu.SemaphoreType.DMA
    return pl.pallas_call(
        functools.partial(body, factor),
        out_shape=(
            jax.ShapeDtypeStruct((256, 512), F32),
            jax.ShapeDtypeStruct((256, 128), F32),
            jax.ShapeDtypeStruct((256, 128), F32),
        ),
        in_specs=[any_space] * 12,
        out_specs=(vmem, vmem, vmem),
        scratch_shapes=[
            pltpu.VMEM((8, T, 512), BF),
            pltpu.VMEM((8, 512, COLS), BF),
            pltpu.VMEM((T, COLS), F32),
            pltpu.VMEM((HEADS, T, 256), BF),
            pltpu.VMEM((HEADS, 256, T), BF),
            pltpu.VMEM((T, 256), BF),
            pltpu.VMEM((T, 256), BF),
            pltpu.VMEM((HD, T), F32),
            pltpu.VMEM((HD, T), F32),
            pltpu.VMEM((HD, T), F32),
            pltpu.VMEM((6, HD, T), BF),
            pltpu.VMEM((3, 2, 4, HD, 512), BF),
            pltpu.VMEM((6, 2, 4, HD, 256), BF),
            pltpu.VMEM((6, 2, 4, HD, 256), BF),
            pltpu.VMEM((6, 4, CUT, 256), BF),
            pltpu.VMEM((6, 4, CUT, 256), BF),
            pltpu.VMEM((6, 4, 2, HD - CUT, 256), BF),
            pltpu.VMEM((6, HD - CUT, 256), BF),
            pltpu.VMEM((6, HD - CUT, 256), F32),
            pltpu.VMEM((T, 512), BF),
            pltpu.VMEM((T, HD), F32),
            pltpu.VMEM((T, HD), F32),
            pltpu.VMEM((HD // 2, T), F32),
            pltpu.VMEM((HD // 2, T), F32),
            dma((12,)),
            dma((MESSAGES,)), dma((MESSAGES,)),
            dma((MESSAGES,)), dma((MESSAGES,)),
            dma((8 * PIECES,)), dma((8 * PIECES,)),
            dma((6, 9)), dma((6, 9)),
        ],
        compiler_params=pltpu.CompilerParams(collective_id=0, has_side_effects=True, vmem_limit_bytes=62 << 20),
        cost_estimate=pl.CostEstimate(flops=25_000_000_000, bytes_accessed=30_000_000, transcendentals=2_000_000),
        name="hvp",
    )(
        tokens, target, w_query, w_key, w_value, t_query, t_key, t_value,
        np.concatenate([cos, cos], axis=1), np.concatenate([-sin, sin], axis=1), cos.T.copy(), sin.T.copy(),
    )


def solution(mesh):
    placed = tuple(P("fsdp", "tp") for _ in range(8))
    return jax.shard_map(
        shards,
        mesh=mesh,
        in_specs=placed,
        out_specs=(P("fsdp", "tp"), P("fsdp", "tp"), P("fsdp", "tp")),
        check_vma=False,
    )
```

```python
import functools
import math

import jax
import jax.numpy as jnp
import numpy as np
from jax import lax
from jax.experimental import pallas as pl
from jax.experimental.pallas import tpu as pltpu
from jax.sharding import PartitionSpec as P

MESH = pl.DeviceIdType.MESH
BF = jnp.bfloat16
F32 = jnp.float32

HD = 128
T = 768
D = 4096
HEADS = 4
R = 256
COLS = 1536
SIGMA = HD ** (-0.5)
LOG2E = 1.4426950408889634


def rope_tables(length, width):
    halfway = width // 2
    frequency = np.exp(np.arange(halfway, dtype=np.float32) * np.float32(-2.0 * math.log(10000.0) / width)).astype(np.float32)
    angles = np.arange(length, dtype=np.float32)[:, None] * frequency[None, :]
    angles = angles.astype(np.float64)
    return np.cos(angles).astype(np.float32), np.sin(angles).astype(np.float32)


def dot(a, b):
    return jnp.dot(a, b, preferred_element_type=F32)


def dot_nt(a, b):
    return lax.dot_general(a, b, (((1,), (1,)), ((), ())), preferred_element_type=F32)


def rope(u, cc, ss):
    return u * cc + pltpu.roll(u, HD // 2, 1) * ss


def unrope(u, cc, ss):
    return u * cc - pltpu.roll(u, HD // 2, 1) * ss


def prepare(project, cc_ref, ss_ref, k2, v2):
    for i in range(T // R):
        rows = slice(i * R, (i + 1) * R)
        cc, ss = cc_ref[rows, :], ss_ref[rows, :]
        k2[rows, :HD] = rope(project("key", 0, rows), cc, ss).astype(BF)
        k2[rows, HD:] = rope(project("d_key", 0, rows), cc, ss).astype(BF)
        v2[rows, :HD] = project("value", 0, rows).astype(BF)
        v2[rows, HD:] = (project("d_value", 0, rows) * (1.0 / SIGMA)).astype(BF)


def prepare_head(h, project, cc_ref, ss_ref, q2, q2t):
    for i in range(T // R):
        rows = slice(i * R, (i + 1) * R)
        cc, ss = cc_ref[rows, :], ss_ref[rows, :]
        both = jnp.concatenate(
            [
                rope(project("d_query", h, rows), cc, ss),
                rope(project("query", h, rows), cc, ss),
            ],
            axis=1,
        )
        q2[h, rows, :] = both.astype(BF)
        q2t[h, :, rows] = both.T.astype(BF)
        yield


def block_steps(h, i, factor, q2, q2t, k2, v2, target, cc_ref, ss_ref, dk1, dk2, dvt, lowt):
    rows = slice(i * R, (i + 1) * R)
    width = (i + 1) * R
    q_both = q2[h, rows, :]
    kr, kd = k2[:width, :HD], k2[:width, HD:]
    vr = v2[:width, :HD]
    s = dot_nt(q_both[:, HD:], kr)
    ds = dot_nt(q_both, k2[:width, :])
    yield
    row = lax.broadcasted_iota(jnp.int32, (R, R), 0)
    col = lax.broadcasted_iota(jnp.int32, (R, R), 1)
    last = jnp.where(col <= row, s[:, i * R:], -1e30)
    s = last if i == 0 else jnp.concatenate([s[:, : i * R], last], axis=1)
    top = jnp.max(s, axis=1, keepdims=True)
    e = jnp.exp2((s - top) * (SIGMA * LOG2E))
    p = e * (1.0 / jnp.sum(e, axis=1, keepdims=True))
    pb = p.astype(BF)
    mixed = dot(pb, v2[:width, :])
    yield
    w = ds - jnp.sum(p * ds, axis=1, keepdims=True)
    pdb = (p * w).astype(BF)
    dmix = dot(pdb, vr) + mixed[:, HD:]
    mix = mixed[:, :HD]
    yield
    err = (mix - target(h, rows).astype(F32)) * factor
    derr = dmix * factor
    both = jnp.concatenate([derr, err], axis=1)
    both_low = both.astype(BF)
    both_t = both.T.astype(BF)
    dp = dot_nt(both_low[:, HD:], vr)
    ddp = dot_nt(both_low, v2[:width, :])
    yield
    delta = jnp.sum(err * mix, axis=1, keepdims=True)
    ddelta = jnp.sum(derr * mix + err * dmix, axis=1, keepdims=True)
    g = dp - delta
    gs = (p * g).astype(BF)
    gd = (p * (w * g + (ddp - ddelta))).astype(BF)
    dvt[:, :width] += dot(both_t[HD:], pdb) + dot(both_t[:HD], pb)
    yield
    dq = dot(gd, kr) * (SIGMA * SIGMA) + dot(gs, kd) * SIGMA
    dk1[:, :width] += dot(q2t[h, HD:, rows], gd)
    dk2[:, :width] += dot(q2t[h, :HD, rows], gs)
    yield
    dq = unrope(dq.astype(BF).astype(F32), cc_ref[rows, :], ss_ref[rows, :])
    lowt[h, :, rows] = dq.T.astype(BF)


def together(*chains):
    chains = list(chains)
    while chains:
        for chain in list(chains):
            if next(chain, chain) is chain:
                chains.remove(chain)


def chained(*chains):
    for chain in chains:
        yield from chain


def clear(dk1, dk2, dvt):
    for ref in (dk1, dk2, dvt):
        ref[...] = jnp.zeros(ref.shape, F32)


def finish_key(cct_ref, sst_ref, dk1, dk2, dvt, lowt):
    dk = dk1[...] * (SIGMA * SIGMA) + dk2[...] * SIGMA
    a, b = dk[: HD // 2], dk[HD // 2:]
    ct, st = cct_ref[...], sst_ref[...]
    lowt[HEADS, : HD // 2, :] = (a * ct + b * st).astype(BF)
    lowt[HEADS, HD // 2:, :] = (b * ct - a * st).astype(BF)
    lowt[HEADS + 1] = (dvt[...] * SIGMA).astype(BF)


def barrier(peers):
    sem = pltpu.get_barrier_semaphore()
    for peer in peers:
        pl.semaphore_signal(sem, inc=1, device_id=peer, device_id_type=MESH)
    pl.semaphore_wait(sem, len(peers))


def remote(src, dst, send, recv, peer):
    return pltpu.make_async_remote_copy(
        src_ref=src, dst_ref=dst, send_sem=send, recv_sem=recv, device_id=peer, device_id_type=MESH
    )


class Place:
    def __init__(self):
        self.f = lax.axis_index("fsdp")
        self.t = lax.axis_index("tp")
        self.core = lax.rem(self.f, 2)
        self.z = lax.rem(lax.div(self.f, 2), 4)
        self.yh = lax.div(self.f, 8)
        self.x = lax.div(self.t, 2)
        self.y = lax.rem(self.t, 2)

    def along(self, base, step):
        return lax.rem(base + step, 4)

    def part_peer(self, j):
        yh, z = lax.rem(self.yh + j // 4, 2), lax.rem(self.z + j % 4, 4)
        return self.fsdp(yh, z, self.core), yh * 4 + z

    def fsdp(self, yh, z, core):
        return {"fsdp": (yh * 4 + z) * 2 + core, "tp": self.t}

    def tp(self, x, y):
        return {"fsdp": self.f, "tp": x * 2 + y}


PIECES = 2
PAIR_ORDER = (0, 1)
CUT = 80
SCATTER_AT = 3


class Ring:
    def __init__(self, r, p, slot, peer, own, send, recv):
        self.slot, self.own, self.send, self.recv = slot, own, send, recv
        right, left, far, q = lax.rem(r + 1, 4), lax.rem(r + 3, 4), lax.rem(r + 2, 4), 1 - p
        to_right, to_left, to_pair = peer(right, p), peer(left, p), peer(r, q)
        self.kinds = {}
        forth = list(range(PIECES))
        back = forth[::-1]

        def add(name, chunk, piece, to, arrives):
            self.kinds[name, piece] = (len(self.kinds), chunk, piece, to, arrives)

        for piece in forth:
            add("right", (r, p), piece, to_right, (left, p))
            add("left", (r, p), piece, to_left, (right, p))
            add("pair", (r, p), piece, to_pair, (r, q))
            add("pair_right", (r, q), piece, to_right, (left, q))
            add("pair_left", (r, q), piece, to_left, (right, q))
        self.top, self.bottom = forth[: PIECES // 2], back[: PIECES // 2]
        for piece in self.top:
            add("far_right", (left, p), piece, to_right, (far, p))
            add("pair_far_right", (left, q), piece, to_right, (far, q))
        for piece in self.bottom:
            add("far_left", (right, p), piece, to_left, (far, p))
            add("pair_far_left", (right, q), piece, to_left, (far, q))

    def make(self, key):
        number, chunk, piece, to, _ = self.kinds[key]
        src = self.own(piece) if key[0] in ("right", "left", "pair") else self.slot(*chunk, piece)
        return remote(src, self.slot(*chunk, piece), self.send.at[number], self.recv.at[number], to)

    def start(self, *key):
        self.make(key).start()

    def arrive(self, *key):
        number, _, piece, to, arrives = self.kinds[key]
        ref = self.slot(*arrives, piece)
        remote(ref, ref, self.send.at[number], self.recv.at[number], to).wait_recv()

    def wait_sends(self):
        for key in self.kinds:
            self.make(key).wait_send()


MESSAGES = 7 * PIECES


NAMES = ("query", "key", "value", "d_query", "d_key", "d_value")
STARTS = {"query": 0, "key": 512, "value": 640, "d_query": 768, "d_key": 1280, "d_value": 1408}
WIDTHS = {"query": 512, "key": 128, "value": 128, "d_query": 512, "d_key": 128, "d_value": 128}


def body(
    factor,
    tokens, target_hbm, w_query, w_key, w_value, t_query, t_key, t_value, cc_hbm, ss_hbm, cct_hbm, sst_hbm,
    out_query, out_key, out_value,
    feat, wbuf, proj, q2, q2t, k2, v2, dk1, dk2, dvt, lowt,
    part, sibr, sums, land_up, land_step, land_low, land_last, done_low, target, cc, ss, cct, sst,
    local_sem, f_send, f_recv, w_send, w_recv, s_send, s_recv, r_send, r_recv,
):
    at = Place()
    sibling = at.fsdp(at.yh, at.z, 1 - at.core)
    f_rows, w_rows_of = T // PIECES, 256 // PIECES

    def f_slot(x, y, piece):
        return feat.at[x * 2 + y, pl.ds(piece * f_rows, f_rows)]

    def w_rows(z, yh, core, piece):
        low = pl.multiple_of(core * 256 + piece * w_rows_of, w_rows_of)
        return wbuf.at[yh * 4 + z, pl.ds(low, w_rows_of)]

    def w_slot(z, yh, piece):
        return w_rows(z, yh, at.core, piece)

    loads = []
    for number, (name, ref) in enumerate(zip(NAMES, (w_query, w_key, w_value, t_query, t_key, t_value))):
        window = wbuf.at[at.yh * 4 + at.z, pl.ds(pl.multiple_of(at.core * 256, 256), 256), pl.ds(STARTS[name], WIDTHS[name])]
        loads.append(pltpu.make_async_copy(ref, window, local_sem.at[number]))
    later = [(tokens, feat.at[at.x * 2 + at.y]), (target_hbm, target), (cc_hbm, cc), (ss_hbm, ss), (cct_hbm, cct), (sst_hbm, sst)]
    late = [pltpu.make_async_copy(src, dst, local_sem.at[6 + number]) for number, (src, dst) in enumerate(later)]
    for load in loads + late:
        load.start()

    ring_f = Ring(at.x, at.y, f_slot, at.tp, lambda piece: tokens.at[pl.ds(piece * f_rows, f_rows)], f_send, f_recv)
    ring_w = Ring(at.z, at.yh, w_slot, lambda z, yh: at.fsdp(yh, z, at.core), lambda piece: w_slot(at.z, at.yh, piece), w_send, w_recv)

    peers = [at.tp(at.along(at.x, 1), at.y), at.tp(at.along(at.x, 3), at.y), at.tp(at.x, 1 - at.y), sibling]
    barrier(peers + [at.part_peer(j)[0] for j in (1, 2, 3, 4)])

    def launch(ring):
        for number in range(PIECES):
            ring.start("right", number)
            ring.start("left", PIECES - 1 - number)
            ring.start("pair", PAIR_ORDER[number])

    launch(ring_f)
    for load in loads:
        load.wait()
    launch(ring_w)

    shared = []

    def share(chunk, piece):
        number = len(shared)
        src, dst = w_rows(*chunk, at.core, piece), w_rows(*chunk, 1 - at.core, piece)
        out = remote(src, src, s_send.at[number], s_recv.at[number], sibling)
        out.start()
        shared.append((out, remote(dst, dst, s_send.at[number], s_recv.at[number], sibling)))

    taken = []

    def take():
        for _, incoming in shared[len(taken):]:
            incoming.wait_recv()
            taken.append(incoming)

    def arrive(name, piece, onward=()):
        for ring in (ring_f, ring_w):
            ring.arrive(name, piece)
            for other in onward:
                if (other, piece) in ring.kinds:
                    ring.start(other, piece)
        kind = ring_w.kinds[name, piece]
        share(kind[4], piece)

    for piece in range(PIECES):
        share((at.z, at.yh), piece)
    proj[...] = jnp.zeros(proj.shape, F32)
    clear(dk1, dk2, dvt)
    forth, back = list(range(PIECES)), list(range(PIECES))[::-1]
    for a, b in zip(forth, back):
        arrive("right", a, ("far_right",))
        arrive("left", b, ("far_left",))
    for piece in forth:
        arrive("pair", piece, ("pair_right", "pair_left"))
    for a, b in zip(ring_f.top, ring_f.bottom):
        arrive("far_right", a)
        arrive("far_left", b)
    late[0].wait()
    take()

    def apart(r, p, ring, pair):
        step = lax.rem(r - ring + 4, 4)
        odd = lax.rem(step, 2)
        return lax.rem(p - pair + 2, 2) * (odd + lax.div(step, 2) * (1 - odd) * 2)

    def project_ready(level):
        def one(t, carry):
            away_f = apart(lax.div(t, 2), lax.rem(t, 2), at.x, at.y)
            away_w = apart(lax.rem(t, 4), lax.div(t, 4), at.z, at.yh)

            @pl.when(jnp.maximum(away_f, away_w) == level)
            def _():
                for i in range(T // R):
                    rows = slice(i * R, (i + 1) * R)
                    proj[rows, :] += dot(feat[t, rows, :], wbuf[t])

            return carry

        lax.fori_loop(0, 8, one, 0)

    project_ready(0)
    for a, b in zip(forth, back):
        arrive("pair_right", a, ("pair_far_right",))
        arrive("pair_left", b, ("pair_far_left",))
    take()
    project_ready(1)
    for a, b in zip(ring_f.top, ring_f.bottom):
        arrive("pair_far_right", a)
        arrive("pair_far_left", b)
    take()
    project_ready(2)
    for load in late[1:]:
        load.wait()

    def project(name, h, rows):
        if WIDTHS[name] == HD:
            return proj[rows, STARTS[name]:STARTS[name] + HD]
        return proj[rows, STARTS[name] + h * HD:STARTS[name] + (h + 1) * HD]

    def target_of(h, rows):
        return target[rows, h * HD:(h + 1) * HD]

    prepare(project, cc, ss, k2, v2)
    together(prepare_head(0, project, cc, ss, q2, q2t))

    keep = pl.ds(pl.multiple_of(at.core * 256, 256), 256)
    give = pl.ds(pl.multiple_of(256 - at.core * 256, 256), 256)

    over = 1 - at.yh
    upper, lower = pl.ds(0, CUT), pl.ds(CUT, HD - CUT)
    across = at.part_peer(4)[0]
    steps = [(j, at.along(at.z, j), at.part_peer(j)[0]) for j in (2, 1, 3)]

    def push(b, number, src, dst, peer):
        return remote(src, dst, r_send.at[b, number], r_recv.at[b, number], peer)

    def swap(b, yh, number):
        return push(b, number, part.at[b % 3, yh, :, :, give], sibr.at[b, yh], sibling)

    def swap_over(b):
        return swap(b, over, 0)

    def swap_own(b):
        return swap(b, at.yh, 9)

    def upper_pair(b):
        return push(b, 1, sums.at[b, over, :, upper], land_up.at[b], across)

    def upper_step(b, j, z, peer):
        return push(b, 1 + j, sums.at[b, at.yh, z, upper], land_step.at[b, j], peer)

    def lower_step(b, j, z, peer):
        return push(b, 4 + j, sums.at[b, :, z, lower], land_low.at[b, j], peer)

    def lower_pair(b):
        return push(b, 8, sums.at[b, over, at.z, lower], land_last.at[b], across)

    def contract_half(b, count, yh):
        low = lowt[b:b + count].reshape(count * HD, T)

        def one(z, carry):
            both = dot(low, feat[yh * 4 + z]).astype(BF)
            for k in range(count):
                part[(b + k) % 3, yh, z] = both[k * HD:(k + 1) * HD]
            return carry

        lax.fori_loop(0, 4, one, 0)

    def add_halves(b, yh, z, rows):
        sums[b, yh, z, rows] = (
            part[b % 3, yh, z, rows, keep].astype(F32) + sibr[b, yh, z, rows].astype(F32)
        ).astype(BF)

    def scatter_upper(b):
        swap_over(b).wait_recv()
        for z in range(4):
            add_halves(b, over, z, upper)
        upper_pair(b).start()

    def scatter_lower(b):
        swap_own(b).wait_recv()
        for step in steps:
            for yh in range(2):
                add_halves(b, yh, step[1], lower)
            lower_step(b, *step).start()
        for z in range(4):
            add_halves(b, at.yh, z, upper)
        for yh in range(2):
            add_halves(b, yh, at.z, lower)

    def scatter(b):
        scatter_upper(b)
        scatter_lower(b)

    def swap_start(b):
        swap_over(b).start()
        swap_own(b).start()

    def swap_sent(b):
        swap_over(b).wait_send()
        swap_own(b).wait_send()

    def relay(b):
        upper_pair(b).wait_recv()
        for step in steps:
            z = step[1]
            sums[b, at.yh, z, upper] = (sums[b, at.yh, z, upper].astype(F32) + land_up[b, z].astype(F32)).astype(BF)
            upper_step(b, *step).start()
        for step in steps:
            lower_step(b, *step).wait_recv()

        def total(yh):
            return (
                sums[b, yh, at.z, lower].astype(F32) + land_low[b, 1, yh].astype(F32)
                + land_low[b, 2, yh].astype(F32) + land_low[b, 3, yh].astype(F32)
            )

        sums[b, over, at.z, lower] = total(over).astype(BF)
        lower_pair(b).start()
        done_low[b] = total(at.yh)

    def collect(b):
        done = sums[b, at.yh, at.z, upper].astype(F32) + land_up[b, at.z].astype(F32)
        for step in steps:
            upper_step(b, *step).wait_recv()
            done = done + land_step[b, step[0]].astype(F32)
        lower_pair(b).wait_recv()
        done = jnp.concatenate([done, done_low[b] + land_last[b].astype(F32)], axis=0).T
        if b < HEADS:
            out_query[:, b * HD:(b + 1) * HD] = done
        elif b == HEADS:
            out_key[...] = done
        else:
            out_value[...] = done

    def attend(h, *others):
        together(
            *[
                block_steps(h, i, factor, q2, q2t, k2, v2, target_of, cc, ss, dk1, dk2, dvt, lowt)
                for i in range(T // R - 1, -1, -1)
            ],
            *others,
            *([prepare_head(h + 1, project, cc, ss, q2, q2t)] if h + 1 < HEADS else []),
        )

    def scatter_inside(b):
        for _ in range(SCATTER_AT):
            yield
        scatter(b)

    def contract_inside(b):
        low = lowt[b]
        for t in range(8):
            part[b % 3, t // 4, t % 4] = dot(low, feat[t]).astype(BF)
            yield

    attend(0)
    attend(1, contract_inside(0))
    swap_start(0)
    attend(2, contract_inside(1), scatter_inside(0))
    swap_start(1)
    attend(3, contract_inside(2), scatter_inside(1))
    swap_start(2)
    finish_key(cct, sst, dk1, dk2, dvt, lowt)
    relay(0)
    scatter(2)
    for b in range(3):
        swap_sent(b)
    contract_half(3, 3, over)
    for b in range(3, HEADS + 2):
        swap_over(b).start()
    contract_half(3, 3, at.yh)
    for b in range(3, HEADS + 2):
        swap_own(b).start()
    relay(1)
    for b in range(3, HEADS + 2):
        scatter_upper(b)
    for b in range(3, HEADS + 2):
        scatter_lower(b)
    relay(2)
    ring_f.wait_sends()
    ring_w.wait_sends()
    for outgoing, _ in shared:
        outgoing.wait_send()
    collect(0)
    collect(1)
    relay(3)
    relay(4)
    relay(5)
    for b in range(2, HEADS + 2):
        collect(b)
    for b in range(HEADS + 2):
        if b > 2:
            swap_sent(b)
        upper_pair(b).wait_send()
        lower_pair(b).wait_send()
        for step in steps:
            upper_step(b, *step).wait_send()
            lower_step(b, *step).wait_send()


def shards(tokens, target, w_query, w_key, w_value, t_query, t_key, t_value):
    factor = (T * 16) ** (-0.5)
    cos, sin = rope_tables(T, HD)
    any_space = pl.BlockSpec(memory_space=pl.ANY)
    vmem = pl.BlockSpec(memory_space=pltpu.VMEM)
    dma = pltpu.SemaphoreType.DMA
    return pl.pallas_call(
        functools.partial(body, factor),
        out_shape=(
            jax.ShapeDtypeStruct((256, 512), F32),
            jax.ShapeDtypeStruct((256, 128), F32),
            jax.ShapeDtypeStruct((256, 128), F32),
        ),
        in_specs=[any_space] * 12,
        out_specs=(vmem, vmem, vmem),
        scratch_shapes=[
            pltpu.VMEM((8, T, 512), BF),
            pltpu.VMEM((8, 512, COLS), BF),
            pltpu.VMEM((T, COLS), F32),
            pltpu.VMEM((HEADS, T, 256), BF),
            pltpu.VMEM((HEADS, 256, T), BF),
            pltpu.VMEM((T, 256), BF),
            pltpu.VMEM((T, 256), BF),
            pltpu.VMEM((HD, T), F32),
            pltpu.VMEM((HD, T), F32),
            pltpu.VMEM((HD, T), F32),
            pltpu.VMEM((6, HD, T), BF),
            pltpu.VMEM((3, 2, 4, HD, 512), BF),
            pltpu.VMEM((6, 2, 4, HD, 256), BF),
            pltpu.VMEM((6, 2, 4, HD, 256), BF),
            pltpu.VMEM((6, 4, CUT, 256), BF),
            pltpu.VMEM((6, 4, CUT, 256), BF),
            pltpu.VMEM((6, 4, 2, HD - CUT, 256), BF),
            pltpu.VMEM((6, HD - CUT, 256), BF),
            pltpu.VMEM((6, HD - CUT, 256), F32),
            pltpu.VMEM((T, 512), BF),
            pltpu.VMEM((T, HD), F32),
            pltpu.VMEM((T, HD), F32),
            pltpu.VMEM((HD // 2, T), F32),
            pltpu.VMEM((HD // 2, T), F32),
            dma((12,)),
            dma((MESSAGES,)), dma((MESSAGES,)),
            dma((MESSAGES,)), dma((MESSAGES,)),
            dma((8 * PIECES,)), dma((8 * PIECES,)),
            dma((6, 10)), dma((6, 10)),
        ],
        compiler_params=pltpu.CompilerParams(collective_id=0, has_side_effects=True, vmem_limit_bytes=62 << 20),
        cost_estimate=pl.CostEstimate(flops=25_000_000_000, bytes_accessed=30_000_000, transcendentals=2_000_000),
        name="hvp",
    )(
        tokens, target, w_query, w_key, w_value, t_query, t_key, t_value,
        np.concatenate([cos, cos], axis=1), np.concatenate([-sin, sin], axis=1), cos.T.copy(), sin.T.copy(),
    )


def solution(mesh):
    placed = tuple(P("fsdp", "tp") for _ in range(8))
    return jax.shard_map(
        shards,
        mesh=mesh,
        in_specs=placed,
        out_specs=(P("fsdp", "tp"), P("fsdp", "tp"), P("fsdp", "tp")),
        check_vma=False,
    )
```
